128 devices in a mesh: ctx: 16 (over z, y_lo, core), exp: 8 (over x, y_hi).
Axes of the slice: x: 4, y: 4 (y_hi: 2, y_lo: 2; y = y_hi * 2 + y_lo), z: 4, core: 2. Of those that a mesh axis runs over, the one named last changes fastest.
Arguments:
- queries: bfloat16 [8, 2048, 2048], P('exp', 'ctx'), may hold values from -18 to 18
- keys: bfloat16 [8, 2048, 2048], P('exp', 'ctx'), may hold values from -18 to 18
- values: bfloat16 [8, 2048, 2048], P('exp', 'ctx'), may hold values from -7 to 7
- segment_ids: int32 [8, 2048], P('exp', 'ctx'), may hold values from 0 to 2, never falling along the last dimension, each value on 1 to 1024 neighbouring positions
- hidden_in: bfloat16 [8, 2048, 2048], P('exp', 'ctx'), may hold values from -6 to 6
- out_weight: bfloat16 [2048, 2048], replicated, may hold values from -0.125 to 0.125
- norm_gain: float32 [2048], replicated, may hold values from 0.25 to 1.75
- expert_ids: int32 [8, 2048, 6], P('exp', 'ctx'), may hold values from 0 to 63, all different within a row; in each aligned block of 128 rows (0 to 127, 128 to 255, ..., all dimensions but the last counted through in order) at most 16 rows name the same one
- gate_codes: int32 [8, 2048, 6], P('exp', 'ctx'), may hold values from 1 to 64
- w_in: bfloat16 [128, 2048, 1408], P(('ctx', 'exp')), may hold values from -0.125 to 0.125
- w_down: bfloat16 [128, 704, 2048], P(('ctx', 'exp')), may hold values from -0.15625 to 0.15625
Outputs:
- layer_out: bfloat16 [8, 2048, 2048], P('exp', 'ctx')
The draws below stay inside these ranges and needn't reach their ends.
Inputs may be any that keep to these rules, and one draw needn't show every extreme that they name: `segment_ids`: segment numbers never fall along a stream; every segment has at most 1024 positions and some segment of each stream has exactly 1024. `expert_ids`: each token names 6 different experts; among the tokens of one device no expert is named more than 16 times, and some device reaches 16.
All inputs are finite; a program needn't handle non-finite values.
Results may differ from the reference program's by a relative error of at most 0.0095.
Values may be sent and summed in bfloat16 or wider, within the bound.
No kernel may reach another device: no remote copies, remote signals or barrier semaphores. Data moves between devices by JAX's collectives and lax.ppermute only.
A program may use at most 128 MiB of HBM per device.

```python
import math
import jax
import jax.numpy as jnp
import numpy as np
from jax import lax

D = 2048
HEADS = 16
HEAD_DIM = 128
FF = 1408
TOPK = 6
TOK_DEV = 128
SEG_COUNT = 3
STREAMS = 8
SEQ = 2048
SEG_MOST = 1024
EXPERTS = 64
HALF = 704
ROUTE_MOST = 16
DEVICES = 128


def drawn_pair(key):
    shape = (STREAMS, SEQ, D)
    base_query = jnp.clip(jax.random.normal(jax.random.fold_in(key, 11), shape, jnp.float32), -4.0, 4.0)
    base_key = jnp.clip(jax.random.normal(jax.random.fold_in(key, 12), shape, jnp.float32), -4.0, 4.0)
    return (base_query, base_key)


def draw_queries(key, part):
    return drawn_pair(key)[0].astype(jnp.bfloat16)


def draw_keys(key, part):
    return drawn_pair(key)[1].astype(jnp.bfloat16)


def draw_values(key, part):
    shape = (STREAMS, SEQ, D)
    base = jnp.clip(jax.random.normal(jax.random.fold_in(key, 21), shape, jnp.float32), -4.0, 4.0)
    offset = jnp.clip(jax.random.normal(jax.random.fold_in(key, 22), (STREAMS, SEQ // TOK_DEV, 1, D), jnp.float32), -3.0, 3.0)
    spread_offset = jnp.broadcast_to(offset, (STREAMS, SEQ // TOK_DEV, TOK_DEV, D)).reshape(shape)
    return (base + spread_offset).astype(jnp.bfloat16)


def with_ends(drawn, own_key, low, high):
    spot = [jax.random.randint(jax.random.fold_in(own_key, axis), (), 0, length) for axis, length in enumerate(drawn.shape)]
    longest = drawn.shape.index(max(drawn.shape))
    next_to = spot[:longest] + [(spot[longest] + 1) % drawn.shape[longest]] + spot[longest + 1:]
    return drawn.at[tuple(spot)].set(low).at[tuple(next_to)].set(high)


def levels(rng, dims, shards, smallest, high):
    def one(dim, shards_of):
        heights = jax.random.uniform(jax.random.fold_in(jax.random.fold_in(rng, 6), dim), (shards_of,), jnp.float32, smallest / len(shards), high / len(shards))
        return jnp.repeat(jnp.exp(heights), dims[dim] // shards_of).reshape((-1,) + (1,) * (len(dims) - dim - 1))

    factor_of = one(*shards[0])
    for cut in shards[1:]:
        factor_of = factor_of * one(*cut)
    return factor_of


def split_up(number_of, total, most, lean):
    loads = [(1 << 20) // math.isqrt(standing ** lean) + 1 for standing in range(2, number_of + 1)]
    surplus, given = total - most - (number_of - 1), [1] * (number_of - 1)
    while surplus > 0:
        candidates = [i for i in range(number_of - 1) if given[i] < most]
        mass, left = sum([loads[i] for i in candidates]), surplus
        for i in candidates:
            extra = min(most - given[i], max(1, left * loads[i] // mass), surplus)
            given[i] = given[i] + extra
            surplus = surplus - extra
    return np.array([most] + given)


def ragged_sizes(key, amount, total, limit, slope):
    if amount == 2:
        one = jax.random.randint(key, (), max(1, total - limit), min(limit, total - 1) + 1)
        return jnp.stack([one, total - one])
    lengths = jnp.asarray(split_up(amount, total, limit, slope), jnp.int32)
    couples = (amount - 1) // 2
    giver, sink = lengths[1:1 + 2 * couples:2], lengths[2:2 + 2 * couples:2]
    margin = jnp.minimum(giver - 1, limit - sink)
    moved = jax.random.randint(jax.random.fold_in(key, 1), (couples,), 0, 1 << 20) % (margin + 1)
    lengths = lengths.at[1:1 + 2 * couples:2].set(giver - moved).at[2:2 + 2 * couples:2].set(sink + moved)
    return lengths[jax.random.permutation(jax.random.fold_in(key, 2), amount)]


def routed_block(rng, own, number, rows, number_of, top, bound, slope):
    sequence = jax.random.permutation(rng, number_of)
    crowded, ordinary = shares(number_of, rows * top, bound, slope, True), shares(number_of, rows * top, bound, slope, False)
    places = jnp.arange(number_of)

    def named(tallies, offset_by):
        used = int((tallies > 0).sum())
        fixed = max(1, used // 4)
        moved = fixed + (places - fixed + offset_by * (used - fixed)) % max(1, number_of - fixed)
        return jnp.zeros((number_of,), jnp.int32).at[sequence[jnp.where(places < fixed, places, moved)]].set(jnp.asarray(tallies, jnp.int32))

    tallies = jnp.where(number % 4 == 0, named(crowded, number // 4), named(ordinary, number - number // 4 - 1))
    mixed = jax.random.permutation(jax.random.fold_in(own, 3), number_of)
    giver, taker = mixed[0:number_of // 2 * 2:2], mixed[1:number_of // 2 * 2:2]
    margin = jnp.minimum(tallies[giver] - 1, bound - tallies[taker]) // 2
    margin = jnp.where((giver == sequence[0]) | (taker == sequence[0]) | (tallies[taker] == 0), 0, jnp.maximum(margin, 0))
    moved = jax.random.randint(jax.random.fold_in(own, 4), (number_of // 2,), 0, 1 << 20) % (margin + 1)
    tallies = tallies.at[giver].add(-moved).at[taker].add(moved)
    labels = jnp.searchsorted(jnp.cumsum(tallies), jnp.arange(rows * top), side="right").astype(jnp.int32)
    table = labels.reshape(top, rows).T
    table = table[jax.random.permutation(jax.random.fold_in(own, 1), rows)]
    offset_by = jax.random.randint(jax.random.fold_in(own, 2), (rows, 1), 0, top)
    return jnp.take_along_axis(table, (jnp.arange(top)[None, :] + offset_by) % top, axis=1)


def shares(number_of, total, most, skew, full):
    loads = [(1 << 20) // math.isqrt(grade ** skew) + 1 for grade in range(1, number_of + 1)]
    largest = most if full else min(most, max(-(-total // number_of), total * loads[0] // sum(loads)))
    least = 1 if total - largest >= number_of - 1 else 0
    counts, spare = [largest] + [least] * (number_of - 1), total - largest - least * (number_of - 1)
    while spare > 0:
        movable = [i for i in range(1, number_of) if counts[i] < largest] or [i for i in range(1, number_of) if counts[i] < most]
        whole, remaining = sum([loads[i] for i in movable]), spare
        for i in movable:
            extra = min(most - counts[i], max(1, remaining * loads[i] // whole), spare)
            counts[i] = counts[i] + extra
            spare = spare - extra
    return np.array(counts)


def normal_values(rng, shape, scale, most, shards=(), kind=jnp.bfloat16):
    drawn = jax.random.normal(rng, shape, jnp.float32) * scale
    if len(shards) > 0:
        drawn = levels(rng, shape, shards, -0.22, 0.18) * drawn
    return jnp.clip(drawn, min=-most, max=most).astype(kind)


def setup_inputs(seed: int = 0) -> dict:
    seeds = jax.random.split(jax.random.key(seed), 12)
    queries = draw_queries(jax.random.fold_in(seeds[11], 71), 0)
    keys = draw_keys(jax.random.fold_in(seeds[11], 71), 0)
    values = draw_values(jax.random.fold_in(seeds[11], 71), 0)
    segment_ids = jax.vmap(lambda own: jnp.searchsorted(jnp.cumsum(ragged_sizes(own, SEG_COUNT, SEQ, SEG_MOST, 1)), jnp.arange(SEQ), side="right"))(jax.random.split(seeds[3], STREAMS)).reshape((STREAMS, SEQ)).astype(jnp.int32)
    hidden_in = normal_values(seeds[4], (STREAMS, SEQ, D), 1.0, 6.0, ((0, 8), (1, 16)))
    out_weight = normal_values(seeds[5], (D, D), D ** -0.5, 0.125)
    norm_gain = jnp.clip(1.0 + 0.15 * jax.random.normal(seeds[6], (D,), jnp.float32), 0.25, 1.75)
    expert_ids_keys = jax.random.split(jax.random.fold_in(seeds[7], 1), STREAMS * SEQ // TOK_DEV)
    expert_ids_turns = jax.random.permutation(jax.random.fold_in(seeds[7], 3), STREAMS * SEQ // TOK_DEV)
    expert_ids = jax.vmap(lambda own, number: routed_block(jax.random.fold_in(seeds[7], 2), own, number, TOK_DEV, EXPERTS, TOPK, ROUTE_MOST, 2))(expert_ids_keys, expert_ids_turns).reshape((STREAMS, SEQ, TOPK))
    gate_codes = with_ends(jax.random.randint(seeds[8], (STREAMS, SEQ, TOPK), 1, 65), jax.random.fold_in(seeds[8], 1), 1, 64).astype(jnp.int32)
    w_in = normal_values(seeds[9], (DEVICES, D, FF), D ** -0.5, 0.125, ((0, 128),))
    w_down = normal_values(seeds[10], (DEVICES, HALF, D), FF ** -0.5, 0.15625, ((0, 128),))
    return dict(queries=queries, keys=keys, values=values, segment_ids=segment_ids, hidden_in=hidden_in, out_weight=out_weight, norm_gain=norm_gain, expert_ids=expert_ids, gate_codes=gate_codes, w_in=w_in, w_down=w_down)


def attend_stream(query_rows, key_rows, value_rows, seg_row):
    scale = HEAD_DIM ** (-0.5)
    query_heads = query_rows.astype(jnp.float32).reshape(SEQ, HEADS, HEAD_DIM)
    key_heads = key_rows.astype(jnp.float32).reshape(SEQ, HEADS, HEAD_DIM)
    value_heads = value_rows.astype(jnp.float32).reshape(SEQ, HEADS, HEAD_DIM)
    position = jnp.arange(SEQ, dtype=jnp.int32)
    block_rows = min(512, SEQ)
    pieces = []
    for block_index in range(SEQ // block_rows):
        first = block_index * block_rows
        query_block = query_heads[first:first + block_rows]
        scores = jnp.einsum('qhd,khd->hqk', query_block, key_heads) * scale
        allowed = (position[None, :] <= position[first:first + block_rows, None]) & (seg_row[None, :] == seg_row[first:first + block_rows, None])
        scores = jnp.where(allowed[None], scores, -jnp.inf)
        row_top = lax.optimization_barrier(jnp.max(scores, axis=-1, keepdims=True))
        probs = jnp.where(allowed[None], jnp.exp(scores - row_top), 0.0)
        total = lax.optimization_barrier(jnp.sum(probs, axis=-1))
        probs_low = lax.optimization_barrier(probs.astype(jnp.bfloat16)).astype(jnp.float32)
        weighted = jnp.einsum('hqk,khd->qhd', probs_low, value_heads)
        pieces.append(weighted / total.T[:, :, None])
    return jnp.concatenate(pieces, axis=0).reshape(SEQ, D).astype(jnp.bfloat16)

def reference(queries, keys, values, segment_ids, hidden_in, out_weight, norm_gain, expert_ids, gate_codes, w_in, w_down):
    attended = jnp.stack([attend_stream(queries[stream], keys[stream], values[stream], segment_ids[stream]) for stream in range(STREAMS)])
    projected = jnp.dot(attended.reshape(STREAMS * SEQ, D), out_weight, preferred_element_type=jnp.float32)
    mixed = (hidden_in.reshape(STREAMS * SEQ, D).astype(jnp.float32) + projected).astype(jnp.bfloat16)
    mixed_wide = mixed.astype(jnp.float32)
    normed = (mixed_wide * lax.rsqrt(lax.optimization_barrier(jnp.mean(mixed_wide * mixed_wide, axis=-1, keepdims=True)) + 1e-06) * norm_gain).astype(jnp.bfloat16)
    token_count = STREAMS * SEQ
    blocks = token_count // TOK_DEV
    normed_pad = jnp.concatenate([normed, jnp.zeros((1, D), jnp.bfloat16)], axis=0)
    flat_ids = expert_ids.reshape(token_count * TOPK).astype(jnp.int32)
    onehot = (flat_ids.reshape(blocks, TOK_DEV * TOPK, 1) == jnp.arange(EXPERTS, dtype=jnp.int32)[None, None, :]).astype(jnp.int32)
    ranks = lax.optimization_barrier(jnp.sum(jnp.cumsum(onehot, axis=1) * onehot, axis=-1)) - 1
    assign = jnp.arange(token_count * TOPK, dtype=jnp.int32)
    slot_flat = (ranks.reshape(-1) + assign // (TOK_DEV * TOPK) * ROUTE_MOST).astype(jnp.int32)
    token_index = (assign // TOPK).astype(jnp.int32)
    table = jnp.full((EXPERTS, blocks * ROUTE_MOST), token_count, jnp.int32).at[flat_ids, slot_flat].set(token_index)
    codes = gate_codes.astype(jnp.float32)
    route_weight = (codes / lax.optimization_barrier(jnp.sum(codes, axis=-1, keepdims=True))).reshape(-1)
    weight_table = jnp.zeros((EXPERTS, blocks * ROUTE_MOST), jnp.float32).at[flat_ids, slot_flat].set(route_weight)
    w_in_pairs = w_in.reshape(EXPERTS, 2, D, FF)
    w_down_pairs = w_down.reshape(EXPERTS, 2, HALF, D)

    def expert_step(running, inputs):
        row_index, row_weight, gate_up, down_rows = inputs
        gathered = normed_pad[row_index]
        expert_sum = jnp.zeros((row_index.shape[0], D), jnp.float32)
        for half_index in range(2):
            inner = jnp.dot(gathered, gate_up[half_index], preferred_element_type=jnp.float32)
            act = (jax.nn.silu(inner[:, :HALF]) * inner[:, HALF:]).astype(jnp.bfloat16)
            part = jnp.dot(act, down_rows[half_index], preferred_element_type=jnp.float32).astype(jnp.bfloat16)
            expert_sum = expert_sum + lax.optimization_barrier(part).astype(jnp.float32)
        running = running.at[row_index].add(row_weight[:, None] * expert_sum)
        return (running, None)
    start_total = jnp.zeros((token_count + 1, D), jnp.float32)
    routed, leftover = lax.scan(expert_step, start_total, (table, weight_table, w_in_pairs, w_down_pairs))
    layer_out = (mixed_wide + routed[:token_count]).astype(jnp.bfloat16)
    return layer_out.reshape(STREAMS, SEQ, D)
```

```python
import jax
import jax.numpy as jnp
from jax import lax
from jax.experimental import pallas as pl
from jax.experimental.pallas import tpu as pltpu
from jax.sharding import PartitionSpec as P

D = 2048
HEADS = 16
HEAD_DIM = 128
TOPK = 6
ROWS = 128
EXPERTS = 64
SLOTS = 16
HALF = 704
SEG_MOST = 1024
SEG_ROWS = 16
PACK_ROWS = 3 * ROWS + SEG_ROWS
Q_BLOCK = 256
NEG_FILL = -1e30

VMEM = pl.BlockSpec(memory_space=pltpu.VMEM)
f32 = jnp.float32
bf16 = jnp.bfloat16


def params(mib):
    return pltpu.CompilerParams(vmem_limit_bytes=mib << 20)


def pack_kernel(q_ref, k_ref, v_ref, seg_ref, out_ref):
    seg = jnp.broadcast_to(seg_ref[...].astype(f32), (SEG_ROWS, ROWS)).astype(bf16)
    for head in range(HEADS):
        lanes = slice(head * HEAD_DIM, (head + 1) * HEAD_DIM)
        out_ref[head, 0:ROWS, :] = q_ref[:, lanes]
        out_ref[head, ROWS : 2 * ROWS, :] = k_ref[:, lanes]
        out_ref[head, 2 * ROWS : 3 * ROWS, :] = v_ref[:, lanes]
        out_ref[head, 3 * ROWS :, :] = seg


def attend_kernel(x_ref, out_ref):
    blocks = x_ref.shape[0]
    seg = x_ref[:, 3 * ROWS :, :].astype(f32)
    first = (jnp.sum(jnp.where(seg < 0.5, 1.0, 0.0)) * (1.0 / SEG_ROWS)).astype(jnp.int32)
    second = (jnp.sum(jnp.where(seg < 1.5, 1.0, 0.0)) * (1.0 / SEG_ROWS)).astype(jnp.int32)
    per = Q_BLOCK // ROWS
    for block in range(blocks // per):
        start = block * per
        low = max(0, start - SEG_MOST // ROWS)
        high = start + per
        width = (high - low) * ROWS
        query = x_ref[start:high, 0:ROWS, :].reshape(Q_BLOCK, HEAD_DIM)
        key = x_ref[low:high, ROWS : 2 * ROWS, :].reshape(width, HEAD_DIM)
        value = x_ref[low:high, 2 * ROWS : 3 * ROWS, :].reshape(width, HEAD_DIM)
        scores = lax.dot_general(
            query, key, (((1,), (1,)), ((), ())), preferred_element_type=f32
        ) * HEAD_DIM ** (-0.5)
        row = start * ROWS + lax.broadcasted_iota(jnp.int32, (Q_BLOCK, 1), 0)
        column = low * ROWS + lax.broadcasted_iota(jnp.int32, (Q_BLOCK, width), 1)
        begin = jnp.where(row < first, 0, jnp.where(row < second, first, second))
        allowed = (column <= row) & (column >= begin)
        scores = jnp.where(allowed, scores, NEG_FILL)
        top = jnp.max(scores, axis=-1, keepdims=True)
        probs = jnp.exp(scores - top)
        total = jnp.sum(probs, axis=-1, keepdims=True)
        mixed = jnp.dot(probs.astype(bf16), value, preferred_element_type=f32)
        out_ref[start:high] = (mixed / total).astype(bf16).reshape(per, ROWS, HEAD_DIM)


def route_kernel(ids_ref, codes_ref, pick_ref, weight_ref):
    expert = lax.broadcasted_iota(jnp.int32, (EXPERTS, ROWS), 0)
    member = jnp.zeros((EXPERTS, ROWS), f32)
    code = jnp.zeros((EXPERTS, ROWS), f32)
    for k in range(TOPK):
        named = expert == ids_ref[k : k + 1, :]
        member = member + jnp.where(named, 1.0, 0.0)
        code = code + jnp.where(named, codes_ref[k : k + 1, :].astype(f32), 0.0)
    earlier = lax.broadcasted_iota(jnp.int32, (ROWS, ROWS), 0) < lax.broadcasted_iota(
        jnp.int32, (ROWS, ROWS), 1
    )
    rank = jnp.dot(
        member.astype(bf16), jnp.where(earlier, 1.0, 0.0).astype(bf16), preferred_element_type=f32
    )
    place = (member * (rank + 1.0)).astype(bf16)

    def spread(table, count):
        rows = EXPERTS * count
        own = lax.broadcasted_iota(jnp.int32, (rows, EXPERTS), 0) // count
        mine = own == lax.broadcasted_iota(jnp.int32, (rows, EXPERTS), 1)
        return jnp.dot(jnp.where(mine, 1.0, 0.0).astype(bf16), table, preferred_element_type=f32)

    def slot(rows):
        return ((lax.broadcasted_iota(jnp.int32, (rows, ROWS), 0) & (SLOTS - 1)) + 1).astype(f32)

    here = spread(place, SLOTS) == slot(EXPERTS * SLOTS)
    pick_ref[...] = jnp.where(here, 1.0, 0.0).astype(bf16)
    both = spread(place, 2 * SLOTS) == slot(EXPERTS * 2 * SLOTS)
    weight_ref[...] = jnp.where(both, spread(code.astype(bf16), 2 * SLOTS), 0.0).astype(bf16)


K_STEPS = 4
SEND_STEPS = 4


def project_kernel(heads_ref, weight_ref, hidden_ref, gain_ref, pick_ref, mixed_ref, send_ref, acc, rows, sems):
    step = pl.program_id(0)
    per = HEADS // K_STEPS
    part = jnp.concatenate([heads_ref[i] for i in range(per)], axis=1)
    product = jnp.dot(part, weight_ref[...], preferred_element_type=f32)

    @pl.when(step == 0)
    def _():
        acc[...] = product

    @pl.when(step > 0)
    def _():
        acc[...] += product

    @pl.when(step == K_STEPS - 1)
    def _():
        mixed = (hidden_ref[...].astype(f32) + acc[...]).astype(bf16)
        mixed_ref[...] = mixed
        wide = mixed.astype(f32)
        scale = lax.rsqrt(jnp.mean(wide * wide, axis=-1, keepdims=True) + 1e-06)
        normed = (wide * scale * gain_ref[...]).astype(bf16)
        count = EXPERTS // SEND_STEPS
        copies = []
        for chunk in range(SEND_STEPS):
            span = slice(chunk * count * SLOTS, (chunk + 1) * count * SLOTS)
            picked = jnp.dot(pick_ref[span, :], normed, preferred_element_type=f32)
            rows[chunk] = picked.astype(bf16).reshape(count, SLOTS, D)
            for half in range(2):
                copy = pltpu.make_async_copy(
                    rows.at[chunk],
                    send_ref.at[pl.ds(chunk * count, count), half],
                    sems.at[chunk, half],
                )
                copy.start()
                copies.append(copy)
        for copy in copies:
            copy.wait()


def expert_kernel(x_ref, in_ref, down_ref, out_ref):
    inner = jnp.dot(x_ref[...], in_ref[...], preferred_element_type=f32)
    gate = inner[:, :HALF]
    up = pltpu.roll(inner, HALF, axis=1)[:, :HALF]
    act = (gate / (1.0 + jnp.exp(-gate)) * up).astype(bf16)
    out_ref[...] = jnp.dot(act, down_ref[...], preferred_element_type=f32).astype(bf16)


def combine_kernel(rows_ref, weight_ref, mixed_ref, out_ref, acc, total):
    step = pl.program_id(0)
    over = (((0,), (0,)), ((), ()))
    weight = weight_ref[...]
    product = lax.dot_general(weight, rows_ref[...], over, preferred_element_type=f32)
    ones = jnp.ones((weight.shape[0], ROWS), bf16)
    count = lax.dot_general(weight, ones, over, preferred_element_type=f32)

    @pl.when(step == 0)
    def _():
        acc[...] = product
        total[...] = count

    @pl.when(step > 0)
    def _():
        acc[...] += product
        total[...] += count

    @pl.when(step == pl.num_programs(0) - 1)
    def _():
        routed = acc[...] / (total[:, 0:1] * 0.5)
        out_ref[...] = (mixed_ref[...].astype(f32) + routed).astype(bf16)


def local(
    queries,
    keys,
    values,
    segment_ids,
    hidden_in,
    out_weight,
    norm_gain,
    expert_ids,
    gate_codes,
    w_in,
    w_down,
):
    owners = 2 * EXPERTS
    shape = jax.ShapeDtypeStruct
    packed = pl.pallas_call(
        pack_kernel,
        out_shape=shape((HEADS, PACK_ROWS, HEAD_DIM), bf16),
        in_specs=[VMEM] * 4,
        out_specs=VMEM,
        name="pack",
    )(queries[0], keys[0], values[0], segment_ids)
    swapped = lax.all_to_all(packed, "ctx", split_axis=0, concat_axis=0, tiled=True)
    attended = pl.pallas_call(
        attend_kernel,
        out_shape=shape((HEADS, ROWS, HEAD_DIM), bf16),
        in_specs=[VMEM],
        out_specs=VMEM,
        compiler_params=params(40),
        name="attend",
    )(swapped)
    heads = lax.all_to_all(attended, "ctx", split_axis=0, concat_axis=0, tiled=True)
    pick, weight = pl.pallas_call(
        route_kernel,
        out_shape=(
            shape((EXPERTS * SLOTS, ROWS), bf16),
            shape((owners * SLOTS, ROWS), bf16),
        ),
        in_specs=[VMEM] * 2,
        out_specs=(VMEM, VMEM),
        name="route",
    )(expert_ids[0].T, gate_codes[0].T)
    per = HEADS // K_STEPS
    mixed, send = pl.pallas_call(
        project_kernel,
        grid=(K_STEPS,),
        out_shape=(
            shape((ROWS, D), bf16),
            shape((EXPERTS, 2, SLOTS, D), bf16),
        ),
        in_specs=[
            pl.BlockSpec((per, ROWS, HEAD_DIM), lambda i: (i, 0, 0)),
            pl.BlockSpec((D // K_STEPS, D), lambda i: (i, 0)),
            pl.BlockSpec((ROWS, D), lambda i: (0, 0)),
            pl.BlockSpec((1, D), lambda i: (0, 0)),
            pl.BlockSpec((EXPERTS * SLOTS, ROWS), lambda i: (0, 0)),
        ],
        out_specs=(
            pl.BlockSpec((ROWS, D), lambda i: (0, 0)),
            pl.BlockSpec(memory_space=pl.ANY),
        ),
        scratch_shapes=[
            pltpu.VMEM((ROWS, D), f32),
            pltpu.VMEM((SEND_STEPS, EXPERTS // SEND_STEPS, SLOTS, D), bf16),
            pltpu.SemaphoreType.DMA((SEND_STEPS, 2)),
        ],
        compiler_params=params(40),
        name="project",
    )(heads, out_weight, hidden_in[0], norm_gain[None], pick)
    arrived = lax.all_to_all(
        send.reshape(owners, SLOTS, D), ("ctx", "exp"), split_axis=0, concat_axis=0, tiled=True
    )
    block = 256
    results = pl.pallas_call(
        expert_kernel,
        grid=(owners * SLOTS // block,),
        out_shape=shape((owners * SLOTS, D), bf16),
        in_specs=[
            pl.BlockSpec((block, D), lambda i: (i, 0)),
            pl.BlockSpec((D, 2 * HALF), lambda i: (0, 0), pipeline_mode=pl.Buffered(1)),
            pl.BlockSpec((HALF, D), lambda i: (0, 0), pipeline_mode=pl.Buffered(1)),
        ],
        out_specs=pl.BlockSpec((block, D), lambda i: (i, 0)),
        compiler_params=params(48),
        name="experts",
    )(arrived.reshape(owners * SLOTS, D), w_in[0], w_down[0])
    returned = lax.all_to_all(
        results.reshape(owners, SLOTS, D), ("ctx", "exp"), split_axis=0, concat_axis=0, tiled=True
    )
    layer_out = pl.pallas_call(
        combine_kernel,
        grid=(owners * SLOTS // block,),
        out_shape=shape((ROWS, D), bf16),
        in_specs=[
            pl.BlockSpec((block, D), lambda i: (i, 0)),
            pl.BlockSpec((block, ROWS), lambda i: (i, 0)),
            pl.BlockSpec((ROWS, D), lambda i: (0, 0)),
        ],
        out_specs=pl.BlockSpec((ROWS, D), lambda i: (0, 0)),
        scratch_shapes=[pltpu.VMEM((ROWS, D), f32), pltpu.VMEM((ROWS, ROWS), f32)],
        compiler_params=params(40),
        name="combine",
    )(returned.reshape(owners * SLOTS, D), weight, mixed)
    return layer_out[None]


def solution(mesh):
    placed = (
        P("exp", "ctx", None),
        P("exp", "ctx", None),
        P("exp", "ctx", None),
        P("exp", "ctx"),
        P("exp", "ctx", None),
        P(),
        P(),
        P("exp", "ctx", None),
        P("exp", "ctx", None),
        P(("ctx", "exp"), None, None),
        P(("ctx", "exp"), None, None),
    )
    return jax.shard_map(
        local, mesh=mesh, in_specs=placed, out_specs=P("exp", "ctx", None), check_vma=False
    )
```

```python
import math

import jax
import jax.numpy as jnp
from jax import lax
from jax.experimental import pallas as pl
from jax.experimental.pallas import tpu as pltpu
from jax.sharding import Mesh
from jax.sharding import PartitionSpec as P

D = 2048
HEADS = 16
HEAD_DIM = 128
TOPK = 6
ROWS = 128
EXPERTS = 64
SLOTS = 16
HALF = 704
SEG_MOST = 1024
SEG_ROWS = 16
PACK_ROWS = 3 * ROWS + SEG_ROWS
Q_BLOCK = 256
X_BLOCK = 512
NEG_FILL = -1e30

VMEM = pl.BlockSpec(memory_space=pltpu.VMEM)
f32 = jnp.float32
bf16 = jnp.bfloat16


SIZES = (4, 2, 2, 4, 2)
AXES = ("z", "yl", "c", "x", "yh")
POSITIONS = ("z", "yl", "c")
STREAM = ("x", "yh")
PLACES = ("z", "yl", "x", "yh")


def moves(target):
    pairs = []
    for number in range(math.prod(SIZES)):
        rest, spot = number, []
        for size in reversed(SIZES):
            spot.append(rest % size)
            rest //= size
        goal = 0
        for size, value in zip(SIZES, target(*reversed(spot))):
            goal = goal * size + value
        pairs.append((number, goal))
    return pairs


def weight_target(z, yl, c, x, yh):
    return (z, 1 - yl, yh, x, c)


def core_target(z, yl, c, x, yh):
    return (z, yl, 1 - c, x, yh)


def params(mib):
    return pltpu.CompilerParams(vmem_limit_bytes=mib << 20)


def pack_kernel(q_ref, k_ref, v_ref, seg_ref, out_ref):
    seg = jnp.broadcast_to(seg_ref[...].astype(f32), (SEG_ROWS, ROWS)).astype(bf16)
    for head in range(HEADS):
        lanes = slice(head * HEAD_DIM, (head + 1) * HEAD_DIM)
        out_ref[head, 0:ROWS, :] = q_ref[:, lanes]
        out_ref[head, ROWS : 2 * ROWS, :] = k_ref[:, lanes]
        out_ref[head, 2 * ROWS : 3 * ROWS, :] = v_ref[:, lanes]
        out_ref[head, 3 * ROWS :, :] = seg


def attend_kernel(x_ref, out_ref):
    blocks = x_ref.shape[0]
    seg = x_ref[:, 3 * ROWS :, :].astype(f32)
    first = (jnp.sum(jnp.where(seg < 0.5, 1.0, 0.0)) * (1.0 / SEG_ROWS)).astype(jnp.int32)
    second = (jnp.sum(jnp.where(seg < 1.5, 1.0, 0.0)) * (1.0 / SEG_ROWS)).astype(jnp.int32)
    per = Q_BLOCK // ROWS
    for block in range(blocks // per):
        start = block * per
        low = max(0, start - SEG_MOST // ROWS)
        high = start + per
        width = (high - low) * ROWS
        query = x_ref[start:high, 0:ROWS, :].reshape(Q_BLOCK, HEAD_DIM)
        key = x_ref[low:high, ROWS : 2 * ROWS, :].reshape(width, HEAD_DIM)
        value = x_ref[low:high, 2 * ROWS : 3 * ROWS, :].reshape(width, HEAD_DIM)
        scores = lax.dot_general(
            query, key, (((1,), (1,)), ((), ())), preferred_element_type=f32
        ) * HEAD_DIM ** (-0.5)
        row = start * ROWS + lax.broadcasted_iota(jnp.int32, (Q_BLOCK, 1), 0)
        column = low * ROWS + lax.broadcasted_iota(jnp.int32, (Q_BLOCK, width), 1)
        begin = jnp.where(row < first, 0, jnp.where(row < second, first, second))
        allowed = (column <= row) & (column >= begin)
        scores = jnp.where(allowed, scores, NEG_FILL)
        top = jnp.max(scores, axis=-1, keepdims=True)
        probs = jnp.exp(scores - top)
        total = jnp.sum(probs, axis=-1, keepdims=True)
        mixed = jnp.dot(probs.astype(bf16), value, preferred_element_type=f32)
        out_ref[start:high] = (mixed / total).astype(bf16).reshape(per, ROWS, HEAD_DIM)


def place_of(expert):
    return (expert & 48) | (8 - (expert & 8)) | ((expert & 3) << 1) | ((expert >> 2) & 1)


def route_kernel(ids_ref, codes_ref, pick_ref, weight_ref):
    expert = lax.broadcasted_iota(jnp.int32, (EXPERTS, ROWS), 0)
    member = jnp.zeros((EXPERTS, ROWS), f32)
    code = jnp.zeros((EXPERTS, ROWS), f32)
    for k in range(TOPK):
        named = expert == place_of(ids_ref[k : k + 1, :])
        member = member + jnp.where(named, 1.0, 0.0)
        code = code + jnp.where(named, codes_ref[k : k + 1, :].astype(f32), 0.0)
    earlier = lax.broadcasted_iota(jnp.int32, (ROWS, ROWS), 0) < lax.broadcasted_iota(
        jnp.int32, (ROWS, ROWS), 1
    )
    rank = jnp.dot(
        member.astype(bf16), jnp.where(earlier, 1.0, 0.0).astype(bf16), preferred_element_type=f32
    )
    rows = EXPERTS * SLOTS
    own = lax.broadcasted_iota(jnp.int32, (rows, EXPERTS), 0) // SLOTS
    mine = own == lax.broadcasted_iota(jnp.int32, (rows, EXPERTS), 1)
    mine = jnp.where(mine, 1.0, 0.0).astype(bf16)
    place = jnp.dot(mine, (member * (rank + 1.0)).astype(bf16), preferred_element_type=f32)
    codes = jnp.dot(mine, code.astype(bf16), preferred_element_type=f32)
    slot = (lax.broadcasted_iota(jnp.int32, (rows, ROWS), 0) & (SLOTS - 1)) + 1
    here = place == slot.astype(f32)
    pick_ref[...] = jnp.where(here, 1.0, 0.0).astype(bf16)
    weight_ref[...] = jnp.where(here, codes, 0.0).astype(bf16)


K_STEPS = 4
SEND_STEPS = 4


def project_kernel(heads_ref, weight_ref, hidden_ref, gain_ref, pick_ref, mixed_ref, send_ref, acc, rows, sems):
    step = pl.program_id(0)
    per = HEADS // K_STEPS
    part = jnp.concatenate([heads_ref[i] for i in range(per)], axis=1)
    product = jnp.dot(part, weight_ref[...], preferred_element_type=f32)

    @pl.when(step == 0)
    def _():
        acc[...] = product

    @pl.when(step > 0)
    def _():
        acc[...] += product

    @pl.when(step == K_STEPS - 1)
    def _():
        mixed = (hidden_ref[...].astype(f32) + acc[...]).astype(bf16)
        mixed_ref[...] = mixed
        wide = mixed.astype(f32)
        scale = lax.rsqrt(jnp.mean(wide * wide, axis=-1, keepdims=True) + 1e-06)
        normed = (wide * scale * gain_ref[...]).astype(bf16)
        count = EXPERTS // SEND_STEPS
        copies = []
        for chunk in range(SEND_STEPS):
            span = slice(chunk * count * SLOTS, (chunk + 1) * count * SLOTS)
            picked = jnp.dot(pick_ref[span, :], normed, preferred_element_type=f32)
            rows[chunk] = picked.astype(bf16).reshape(count, SLOTS, D)
            copy = pltpu.make_async_copy(
                rows.at[chunk], send_ref.at[pl.ds(chunk * count, count)], sems.at[chunk]
            )
            copy.start()
            copies.append(copy)
        for copy in copies:
            copy.wait()


def expert_kernel(x_any, in_a, in_b, down_a, down_b, out_any, x, w_in, w_down, act, out, sems, out_sems):
    blocks = x.shape[0]
    copies = [pltpu.make_async_copy(x_any, x, sems.at[0])]
    for half, (source, down) in enumerate(((in_a, down_a), (in_b, down_b))):
        copies.append(pltpu.make_async_copy(source, w_in.at[half], sems.at[1 + half]))
    for half, down in enumerate((down_a, down_b)):
        copies.append(pltpu.make_async_copy(down, w_down.at[half], sems.at[3 + half]))
    for copy in copies:
        copy.start()
    copies[0].wait()
    for half in range(2):
        copies[1 + half].wait()
        for block in range(blocks):
            inner = jnp.dot(x[block], w_in[half], preferred_element_type=f32)
            gate = inner[:, :HALF]
            up = pltpu.roll(inner, HALF, axis=1)[:, :HALF]
            act[half, block] = (gate / (1.0 + jnp.exp(-gate)) * up).astype(bf16)
    copies[3].wait()
    copies[4].wait()
    sends = []
    for block in range(blocks):
        total = jnp.dot(act[0, block], w_down[0], preferred_element_type=f32)
        total = total + jnp.dot(act[1, block], w_down[1], preferred_element_type=f32)
        out[block] = total.astype(bf16)
        send = pltpu.make_async_copy(out.at[block], out_any.at[block], out_sems.at[block])
        send.start()
        sends.append(send)
    for send in sends:
        send.wait()


def combine_kernel(rows_ref, weight_ref, mixed_ref, out_ref, acc, total):
    step = pl.program_id(0)
    over = (((0,), (0,)), ((), ()))
    weight = weight_ref[...]
    product = lax.dot_general(weight, rows_ref[...], over, preferred_element_type=f32)
    ones = jnp.ones((weight.shape[0], ROWS), bf16)
    count = lax.dot_general(weight, ones, over, preferred_element_type=f32)

    @pl.when(step == 0)
    def _():
        acc[...] = product
        total[...] = count

    @pl.when(step > 0)
    def _():
        acc[...] += product
        total[...] += count

    @pl.when(step == pl.num_programs(0) - 1)
    def _():
        routed = acc[...] / total[:, 0:1]
        out_ref[...] = (mixed_ref[...].astype(f32) + routed).astype(bf16)


def local(
    queries,
    keys,
    values,
    segment_ids,
    hidden_in,
    out_weight,
    norm_gain,
    expert_ids,
    gate_codes,
    w_in,
    w_down,
):
    shape = jax.ShapeDtypeStruct
    moved_in = lax.ppermute(w_in[0], AXES, moves(weight_target))
    moved_down = lax.ppermute(w_down[0], AXES, moves(weight_target))
    other_in = lax.ppermute(moved_in, AXES, moves(core_target))
    other_down = lax.ppermute(moved_down, AXES, moves(core_target))
    packed = pl.pallas_call(
        pack_kernel,
        out_shape=shape((HEADS, PACK_ROWS, HEAD_DIM), bf16),
        in_specs=[VMEM] * 4,
        out_specs=VMEM,
        name="pack",
    )(queries[0], keys[0], values[0], segment_ids)
    swapped = lax.all_to_all(packed, POSITIONS, split_axis=0, concat_axis=0, tiled=True)
    attended = pl.pallas_call(
        attend_kernel,
        out_shape=shape((HEADS, ROWS, HEAD_DIM), bf16),
        in_specs=[VMEM],
        out_specs=VMEM,
        compiler_params=params(40),
        name="attend",
    )(swapped)
    heads = lax.all_to_all(attended, POSITIONS, split_axis=0, concat_axis=0, tiled=True)
    pick, weight = pl.pallas_call(
        route_kernel,
        out_shape=(
            shape((EXPERTS * SLOTS, ROWS), bf16),
            shape((EXPERTS * SLOTS, ROWS), bf16),
        ),
        in_specs=[VMEM] * 2,
        out_specs=(VMEM, VMEM),
        name="route",
    )(expert_ids[0].T, gate_codes[0].T)
    per = HEADS // K_STEPS
    mixed, send = pl.pallas_call(
        project_kernel,
        grid=(K_STEPS,),
        out_shape=(
            shape((ROWS, D), bf16),
            shape((EXPERTS, SLOTS, D), bf16),
        ),
        in_specs=[
            pl.BlockSpec((per, ROWS, HEAD_DIM), lambda i: (i, 0, 0)),
            pl.BlockSpec((D // K_STEPS, D), lambda i: (i, 0)),
            pl.BlockSpec((ROWS, D), lambda i: (0, 0)),
            pl.BlockSpec((1, D), lambda i: (0, 0)),
            pl.BlockSpec((EXPERTS * SLOTS, ROWS), lambda i: (0, 0)),
        ],
        out_specs=(
            pl.BlockSpec((ROWS, D), lambda i: (0, 0)),
            pl.BlockSpec(memory_space=pltpu.HBM),
        ),
        scratch_shapes=[
            pltpu.VMEM((ROWS, D), f32),
            pltpu.VMEM((SEND_STEPS, EXPERTS // SEND_STEPS, SLOTS, D), bf16),
            pltpu.SemaphoreType.DMA((SEND_STEPS,)),
        ],
        compiler_params=params(40),
        name="project",
    )(heads, out_weight, hidden_in[0], norm_gain[None], pick)
    arrived = lax.all_to_all(send, PLACES, split_axis=0, concat_axis=0, tiled=True)
    blocks = EXPERTS * SLOTS // X_BLOCK
    anywhere = pl.BlockSpec(memory_space=pl.ANY)
    results = pl.pallas_call(
        expert_kernel,
        out_shape=shape((blocks, X_BLOCK, D), bf16),
        in_specs=[anywhere] * 5,
        out_specs=anywhere,
        scratch_shapes=[
            pltpu.VMEM((blocks, X_BLOCK, D), bf16),
            pltpu.VMEM((2, D, 2 * HALF), bf16),
            pltpu.VMEM((2, HALF, D), bf16),
            pltpu.VMEM((2, blocks, X_BLOCK, HALF), bf16),
            pltpu.VMEM((blocks, X_BLOCK, D), bf16),
            pltpu.SemaphoreType.DMA((5,)),
            pltpu.SemaphoreType.DMA((blocks,)),
        ],
        compiler_params=params(56),
        name="experts",
    )(arrived.reshape(blocks, X_BLOCK, D), moved_in, other_in, moved_down, other_down)
    returned = lax.all_to_all(
        results.reshape(EXPERTS, SLOTS, D), PLACES, split_axis=0, concat_axis=0, tiled=True
    )
    block = 256
    layer_out = pl.pallas_call(
        combine_kernel,
        grid=(EXPERTS * SLOTS // block,),
        out_shape=shape((ROWS, D), bf16),
        in_specs=[
            pl.BlockSpec((block, D), lambda i: (i, 0)),
            pl.BlockSpec((block, ROWS), lambda i: (i, 0)),
            pl.BlockSpec((ROWS, D), lambda i: (0, 0)),
        ],
        out_specs=pl.BlockSpec((ROWS, D), lambda i: (0, 0)),
        scratch_shapes=[pltpu.VMEM((ROWS, D), f32), pltpu.VMEM((ROWS, ROWS), f32)],
        compiler_params=params(40),
        name="combine",
    )(returned.reshape(EXPERTS * SLOTS, D), weight, mixed)
    return layer_out[None]


def solution(mesh):
    parts = Mesh(mesh.devices.reshape(SIZES), AXES)
    rows = P(STREAM, POSITIONS, None)
    owned = P((*POSITIONS, *STREAM), None, None)
    placed = (rows, rows, rows, P(STREAM, POSITIONS), rows, P(), P(), rows, rows, owned, owned)
    return jax.shard_map(local, mesh=parts, in_specs=placed, out_specs=rows, check_vma=False)
```

```python
import math

import jax
import jax.numpy as jnp
from jax import lax
from jax.experimental import pallas as pl
from jax.experimental.pallas import tpu as pltpu
from jax.sharding import Mesh
from jax.sharding import PartitionSpec as P

D = 2048
HEADS = 16
HEAD_DIM = 128
TOPK = 6
ROWS = 128
EXPERTS = 64
SLOTS = 16
HALF = 704
SEG_MOST = 1024
SEG_ROWS = 16
PACK_ROWS = 3 * ROWS + SEG_ROWS
Q_BLOCK = 256
X_BLOCK = 512
PIECES = (256, 384, 448, 960)
NEG_FILL = -1e30

VMEM = pl.BlockSpec(memory_space=pltpu.VMEM)
f32 = jnp.float32
bf16 = jnp.bfloat16


SIZES = (4, 2, 2, 4, 2)
AXES = ("z", "yl", "c", "x", "yh")
POSITIONS = ("z", "yl", "c")
STREAM = ("x", "yh")
PLACES = ("z", "yl", "x", "yh")


def moves(target):
    pairs = []
    for number in range(math.prod(SIZES)):
        rest, spot = number, []
        for size in reversed(SIZES):
            spot.append(rest % size)
            rest //= size
        goal = 0
        for size, value in zip(SIZES, target(*reversed(spot))):
            goal = goal * size + value
        pairs.append((number, goal))
    return pairs


def weight_target(z, yl, c, x, yh):
    return (z, 1 - yl, yh, x, c)


def core_target(z, yl, c, x, yh):
    return (z, yl, 1 - c, x, yh)


def params(mib):
    return pltpu.CompilerParams(vmem_limit_bytes=mib << 20)


def pack_kernel(q_ref, k_ref, v_ref, seg_ref, out_ref):
    seg = jnp.broadcast_to(seg_ref[...].astype(f32), (SEG_ROWS, ROWS)).astype(bf16)
    for head in range(HEADS):
        lanes = slice(head * HEAD_DIM, (head + 1) * HEAD_DIM)
        out_ref[head, 0:ROWS, :] = q_ref[:, lanes]
        out_ref[head, ROWS : 2 * ROWS, :] = k_ref[:, lanes]
        out_ref[head, 2 * ROWS : 3 * ROWS, :] = v_ref[:, lanes]
        out_ref[head, 3 * ROWS :, :] = seg


def attend_kernel(x_ref, out_ref):
    blocks = x_ref.shape[0]
    seg = x_ref[:, 3 * ROWS :, :].astype(f32)
    first = (jnp.sum(jnp.where(seg < 0.5, 1.0, 0.0)) * (1.0 / SEG_ROWS)).astype(jnp.int32)
    second = (jnp.sum(jnp.where(seg < 1.5, 1.0, 0.0)) * (1.0 / SEG_ROWS)).astype(jnp.int32)
    per = Q_BLOCK // ROWS
    for block in range(blocks // per):
        start = block * per
        low = max(0, start - SEG_MOST // ROWS)
        high = start + per
        width = (high - low) * ROWS
        query = x_ref[start:high, 0:ROWS, :].reshape(Q_BLOCK, HEAD_DIM)
        key = x_ref[low:high, ROWS : 2 * ROWS, :].reshape(width, HEAD_DIM)
        value = x_ref[low:high, 2 * ROWS : 3 * ROWS, :].reshape(width, HEAD_DIM)
        scores = lax.dot_general(
            query, key, (((1,), (1,)), ((), ())), preferred_element_type=f32
        ) * HEAD_DIM ** (-0.5)
        row = start * ROWS + lax.broadcasted_iota(jnp.int32, (Q_BLOCK, 1), 0)
        column = low * ROWS + lax.broadcasted_iota(jnp.int32, (Q_BLOCK, width), 1)
        begin = jnp.where(row < first, 0, jnp.where(row < second, first, second))
        allowed = (column <= row) & (column >= begin)
        scores = jnp.where(allowed, scores, NEG_FILL)
        top = jnp.max(scores, axis=-1, keepdims=True)
        probs = jnp.exp(scores - top)
        total = jnp.sum(probs, axis=-1, keepdims=True)
        mixed = jnp.dot(probs.astype(bf16), value, preferred_element_type=f32)
        out_ref[start:high] = (mixed / total).astype(bf16).reshape(per, ROWS, HEAD_DIM)


def place_of(expert):
    return (expert & 48) | (8 - (expert & 8)) | ((expert & 3) << 1) | ((expert >> 2) & 1)


def route_kernel(ids_ref, codes_ref, pick_ref, weight_ref):
    expert = lax.broadcasted_iota(jnp.int32, (EXPERTS, ROWS), 0)
    member = jnp.zeros((EXPERTS, ROWS), f32)
    code = jnp.zeros((EXPERTS, ROWS), f32)
    for k in range(TOPK):
        named = expert == place_of(ids_ref[k : k + 1, :])
        member = member + jnp.where(named, 1.0, 0.0)
        code = code + jnp.where(named, codes_ref[k : k + 1, :].astype(f32), 0.0)
    earlier = lax.broadcasted_iota(jnp.int32, (ROWS, ROWS), 0) < lax.broadcasted_iota(
        jnp.int32, (ROWS, ROWS), 1
    )
    rank = jnp.dot(
        member.astype(bf16), jnp.where(earlier, 1.0, 0.0).astype(bf16), preferred_element_type=f32
    )
    rows = EXPERTS * SLOTS
    own = lax.broadcasted_iota(jnp.int32, (rows, EXPERTS), 0) // SLOTS
    mine = own == lax.broadcasted_iota(jnp.int32, (rows, EXPERTS), 1)
    mine = jnp.where(mine, 1.0, 0.0).astype(bf16)
    place = jnp.dot(mine, (member * (rank + 1.0)).astype(bf16), preferred_element_type=f32)
    codes = jnp.dot(mine, code.astype(bf16), preferred_element_type=f32)
    slot = (lax.broadcasted_iota(jnp.int32, (rows, ROWS), 0) & (SLOTS - 1)) + 1
    here = place == slot.astype(f32)
    pick_ref[...] = jnp.where(here, 1.0, 0.0).astype(bf16)
    weight_ref[...] = jnp.where(here, codes, 0.0).astype(bf16)


K_STEPS = 4
SEND_STEPS = 4


def project_kernel(heads_ref, weight_ref, hidden_ref, gain_ref, pick_ref, mixed_ref, send_ref, acc, rows, sems):
    step = pl.program_id(0)
    per = HEADS // K_STEPS
    part = jnp.concatenate([heads_ref[i] for i in range(per)], axis=1)
    product = jnp.dot(part, weight_ref[...], preferred_element_type=f32)

    @pl.when(step == 0)
    def _():
        acc[...] = product

    @pl.when(step > 0)
    def _():
        acc[...] += product

    @pl.when(step == K_STEPS - 1)
    def _():
        mixed = (hidden_ref[...].astype(f32) + acc[...]).astype(bf16)
        mixed_ref[...] = mixed
        wide = mixed.astype(f32)
        scale = lax.rsqrt(jnp.mean(wide * wide, axis=-1, keepdims=True) + 1e-06)
        normed = (wide * scale * gain_ref[...]).astype(bf16)
        count = EXPERTS // SEND_STEPS
        copies = []
        for chunk in range(SEND_STEPS):
            span = slice(chunk * count * SLOTS, (chunk + 1) * count * SLOTS)
            picked = jnp.dot(pick_ref[span, :], normed, preferred_element_type=f32)
            rows[chunk] = picked.astype(bf16).reshape(count, SLOTS, D)
            copy = pltpu.make_async_copy(
                rows.at[chunk], send_ref.at[pl.ds(chunk * count, count)], sems.at[chunk]
            )
            copy.start()
            copies.append(copy)
        for copy in copies:
            copy.wait()


def inner_kernel(*refs):
    pieces = len(PIECES)
    x_any, first, second = refs[0], refs[1 : 1 + pieces], refs[1 + pieces : 1 + 2 * pieces]
    act, x, w_in, sems = refs[1 + 2 * pieces :]
    load = pltpu.make_async_copy(x_any, x, sems.at[2, 0])
    load.start()
    copies = []
    for half, parts in enumerate((first, second)):
        start = 0
        for number, (part, count) in enumerate(zip(parts, PIECES)):
            goal = w_in.at[half, pl.ds(start, count)]
            copies.append(pltpu.make_async_copy(part, goal, sems.at[half, number]))
            start += count
    for copy in copies:
        copy.start()
    load.wait()
    for half in range(2):
        for number in range(pieces):
            copies[half * pieces + number].wait()
        for block in range(x.shape[0]):
            inner = jnp.dot(x[block], w_in[half], preferred_element_type=f32)
            gate = inner[:, :HALF]
            up = pltpu.roll(inner, HALF, axis=1)[:, :HALF]
            act[half, block] = (gate / (1.0 + jnp.exp(-gate)) * up).astype(bf16)


def down_kernel(act, down_a, down_b, out_any, w_down, out, sems, out_sems):
    copies = []
    for half, down in enumerate((down_a, down_b)):
        copies.append(pltpu.make_async_copy(down, w_down.at[half], sems.at[half]))
    for copy in copies:
        copy.start()
    for copy in copies:
        copy.wait()
    sends = []
    for block in range(out.shape[0]):
        total = jnp.dot(act[0, block], w_down[0], preferred_element_type=f32)
        total = total + jnp.dot(act[1, block], w_down[1], preferred_element_type=f32)
        out[block] = total.astype(bf16)
        send = pltpu.make_async_copy(out.at[block], out_any.at[block], out_sems.at[block])
        send.start()
        sends.append(send)
    for send in sends:
        send.wait()


def combine_kernel(rows_ref, weight_ref, mixed_ref, out_ref, acc, total):
    step = pl.program_id(0)
    over = (((0,), (0,)), ((), ()))
    weight = weight_ref[...]
    product = lax.dot_general(weight, rows_ref[...], over, preferred_element_type=f32)
    ones = jnp.ones((weight.shape[0], ROWS), bf16)
    count = lax.dot_general(weight, ones, over, preferred_element_type=f32)

    @pl.when(step == 0)
    def _():
        acc[...] = product
        total[...] = count

    @pl.when(step > 0)
    def _():
        acc[...] += product
        total[...] += count

    @pl.when(step == pl.num_programs(0) - 1)
    def _():
        routed = acc[...] / total[:, 0:1]
        out_ref[...] = (mixed_ref[...].astype(f32) + routed).astype(bf16)


def local(
    queries,
    keys,
    values,
    segment_ids,
    hidden_in,
    out_weight,
    norm_gain,
    expert_ids,
    gate_codes,
    w_in,
    w_down,
):
    shape = jax.ShapeDtypeStruct
    gate_up, start, moved, other = w_in[0], 0, [], []
    for count in PIECES:
        piece = lax.slice_in_dim(gate_up, start, start + count)
        moved.append(lax.ppermute(piece, AXES, moves(weight_target)))
        other.append(lax.ppermute(moved[-1], AXES, moves(core_target)))
        start += count
    moved_down = lax.ppermute(w_down[0], AXES, moves(weight_target))
    other_down = lax.ppermute(moved_down, AXES, moves(core_target))
    packed = pl.pallas_call(
        pack_kernel,
        out_shape=shape((HEADS, PACK_ROWS, HEAD_DIM), bf16),
        in_specs=[VMEM] * 4,
        out_specs=VMEM,
        compiler_params=params(60),
        name="pack",
    )(queries[0], keys[0], values[0], segment_ids)
    swapped = lax.all_to_all(packed, POSITIONS, split_axis=0, concat_axis=0, tiled=True)
    attended = pl.pallas_call(
        attend_kernel,
        out_shape=shape((HEADS, ROWS, HEAD_DIM), bf16),
        in_specs=[VMEM],
        out_specs=VMEM,
        compiler_params=params(40),
        name="attend",
    )(swapped)
    heads = lax.all_to_all(attended, POSITIONS, split_axis=0, concat_axis=0, tiled=True)
    pick, weight = pl.pallas_call(
        route_kernel,
        out_shape=(
            shape((EXPERTS * SLOTS, ROWS), bf16),
            shape((EXPERTS * SLOTS, ROWS), bf16),
        ),
        in_specs=[VMEM] * 2,
        out_specs=(VMEM, VMEM),
        compiler_params=params(60),
        name="route",
    )(expert_ids[0].T, gate_codes[0].T)
    per = HEADS // K_STEPS
    mixed, send = pl.pallas_call(
        project_kernel,
        grid=(K_STEPS,),
        out_shape=(
            shape((ROWS, D), bf16),
            shape((EXPERTS, SLOTS, D), bf16),
        ),
        in_specs=[
            pl.BlockSpec((per, ROWS, HEAD_DIM), lambda i: (i, 0, 0)),
            pl.BlockSpec((D // K_STEPS, D), lambda i: (i, 0)),
            pl.BlockSpec((ROWS, D), lambda i: (0, 0)),
            pl.BlockSpec((1, D), lambda i: (0, 0)),
            pl.BlockSpec((EXPERTS * SLOTS, ROWS), lambda i: (0, 0)),
        ],
        out_specs=(
            pl.BlockSpec((ROWS, D), lambda i: (0, 0)),
            pl.BlockSpec(memory_space=pltpu.HBM),
        ),
        scratch_shapes=[
            pltpu.VMEM((ROWS, D), f32),
            pltpu.VMEM((SEND_STEPS, EXPERTS // SEND_STEPS, SLOTS, D), bf16),
            pltpu.SemaphoreType.DMA((SEND_STEPS,)),
        ],
        compiler_params=params(55),
        name="project",
    )(heads, out_weight, hidden_in[0], norm_gain[None], pick)
    arrived = lax.all_to_all(send, PLACES, split_axis=0, concat_axis=0, tiled=True)
    blocks = EXPERTS * SLOTS // X_BLOCK
    anywhere = pl.BlockSpec(memory_space=pl.ANY)
    act = pl.pallas_call(
        inner_kernel,
        out_shape=shape((2, blocks, X_BLOCK, HALF), bf16),
        in_specs=[anywhere] * (1 + 2 * len(PIECES)),
        out_specs=VMEM,
        scratch_shapes=[
            pltpu.VMEM((blocks, X_BLOCK, D), bf16),
            pltpu.VMEM((2, D, 2 * HALF), bf16),
            pltpu.SemaphoreType.DMA((3, len(PIECES))),
        ],
        compiler_params=params(58),
        name="inner",
    )(arrived.reshape(blocks, X_BLOCK, D), *moved, *other)
    results = pl.pallas_call(
        down_kernel,
        out_shape=shape((blocks, X_BLOCK, D), bf16),
        in_specs=[VMEM, anywhere, anywhere],
        out_specs=anywhere,
        scratch_shapes=[
            pltpu.VMEM((2, HALF, D), bf16),
            pltpu.VMEM((blocks, X_BLOCK, D), bf16),
            pltpu.SemaphoreType.DMA((2,)),
            pltpu.SemaphoreType.DMA((blocks,)),
        ],
        compiler_params=params(58),
        name="down",
    )(act, moved_down, other_down)
    returned = lax.all_to_all(
        results.reshape(EXPERTS, SLOTS, D), PLACES, split_axis=0, concat_axis=0, tiled=True
    )
    block = 256
    layer_out = pl.pallas_call(
        combine_kernel,
        grid=(EXPERTS * SLOTS // block,),
        out_shape=shape((ROWS, D), bf16),
        in_specs=[
            pl.BlockSpec((block, D), lambda i: (i, 0)),
            pl.BlockSpec((block, ROWS), lambda i: (i, 0)),
            pl.BlockSpec((ROWS, D), lambda i: (0, 0)),
        ],
        out_specs=pl.BlockSpec((ROWS, D), lambda i: (0, 0)),
        scratch_shapes=[pltpu.VMEM((ROWS, D), f32), pltpu.VMEM((ROWS, ROWS), f32)],
        compiler_params=params(12),
        name="combine",
    )(returned.reshape(EXPERTS * SLOTS, D), weight, mixed)
    return layer_out[None]


def solution(mesh):
    parts = Mesh(mesh.devices.reshape(SIZES), AXES)
    rows = P(STREAM, POSITIONS, None)
    owned = P((*POSITIONS, *STREAM), None, None)
    placed = (rows, rows, rows, P(STREAM, POSITIONS), rows, P(), P(), rows, rows, owned, owned)
    return jax.shard_map(local, mesh=parts, in_specs=placed, out_specs=rows, check_vma=False)
```

```python
import math

import jax
import jax.numpy as jnp
from jax import lax
from jax.experimental import pallas as pl
from jax.experimental.pallas import tpu as pltpu
from jax.sharding import Mesh
from jax.sharding import PartitionSpec as P

D = 2048
HEADS = 16
HEAD_DIM = 128
TOPK = 6
ROWS = 128
EXPERTS = 64
SLOTS = 16
HALF = 704
SEG_MOST = 1024
SEG_ROWS = 16
PACK_ROWS = 3 * ROWS + SEG_ROWS
Q_BLOCK = 256
X_BLOCK = 512
PIECES = (256, 384, 448, 960)
SPOTS = 16
Y_SIZE = 4
NEG_FILL = -1e30

VMEM = pl.BlockSpec(memory_space=pltpu.VMEM)
f32 = jnp.float32
bf16 = jnp.bfloat16


SIZES = (4, 2, 2, 4, 2)
AXES = ("z", "yl", "c", "x", "yh")
POSITIONS = ("z", "yl", "c")
STREAM = ("x", "yh")
PLACES = ("z", "yl", "x", "yh")


def moves(target):
    pairs = []
    for number in range(math.prod(SIZES)):
        rest, spot = number, []
        for size in reversed(SIZES):
            spot.append(rest % size)
            rest //= size
        goal = 0
        for size, value in zip(SIZES, target(*reversed(spot))):
            goal = goal * size + value
        pairs.append((number, goal))
    return pairs


def weight_target(z, yl, c, x, yh):
    return (z, 1 - yl, yh, x, c)


def core_target(z, yl, c, x, yh):
    return (z, yl, 1 - c, x, yh)


def params(mib):
    return pltpu.CompilerParams(vmem_limit_bytes=mib << 20)


def pack_kernel(q_ref, k_ref, v_ref, seg_ref, out_ref):
    seg = jnp.broadcast_to(seg_ref[...].astype(f32), (SEG_ROWS, ROWS)).astype(bf16)
    for head in range(HEADS):
        lanes = slice(head * HEAD_DIM, (head + 1) * HEAD_DIM)
        out_ref[head, 0:ROWS, :] = q_ref[:, lanes]
        out_ref[head, ROWS : 2 * ROWS, :] = k_ref[:, lanes]
        out_ref[head, 2 * ROWS : 3 * ROWS, :] = v_ref[:, lanes]
        out_ref[head, 3 * ROWS :, :] = seg


def attend_kernel(x_ref, out_ref):
    blocks = x_ref.shape[0]
    seg = x_ref[:, 3 * ROWS :, :].astype(f32)
    first = (jnp.sum(jnp.where(seg < 0.5, 1.0, 0.0)) * (1.0 / SEG_ROWS)).astype(jnp.int32)
    second = (jnp.sum(jnp.where(seg < 1.5, 1.0, 0.0)) * (1.0 / SEG_ROWS)).astype(jnp.int32)
    per = Q_BLOCK // ROWS
    for block in range(blocks // per):
        start = block * per
        low = max(0, start - SEG_MOST // ROWS)
        high = start + per
        width = (high - low) * ROWS
        query = x_ref[start:high, 0:ROWS, :].reshape(Q_BLOCK, HEAD_DIM)
        key = x_ref[low:high, ROWS : 2 * ROWS, :].reshape(width, HEAD_DIM)
        value = x_ref[low:high, 2 * ROWS : 3 * ROWS, :].reshape(width, HEAD_DIM)
        scores = lax.dot_general(
            query, key, (((1,), (1,)), ((), ())), preferred_element_type=f32
        ) * HEAD_DIM ** (-0.5)
        row = start * ROWS + lax.broadcasted_iota(jnp.int32, (Q_BLOCK, 1), 0)
        column = low * ROWS + lax.broadcasted_iota(jnp.int32, (Q_BLOCK, width), 1)
        begin = jnp.where(row < first, 0, jnp.where(row < second, first, second))
        allowed = (column <= row) & (column >= begin)
        scores = jnp.where(allowed, scores, NEG_FILL)
        top = jnp.max(scores, axis=-1, keepdims=True)
        probs = jnp.exp(scores - top)
        total = jnp.sum(probs, axis=-1, keepdims=True)
        mixed = jnp.dot(probs.astype(bf16), value, preferred_element_type=f32)
        out_ref[start:high] = (mixed / total).astype(bf16).reshape(per, ROWS, HEAD_DIM)


def place_of(expert):
    return (expert & 48) | (8 - (expert & 8)) | ((expert & 3) << 1) | ((expert >> 2) & 1)


def route_kernel(ids_ref, codes_ref, pick_ref, weight_ref):
    expert = lax.broadcasted_iota(jnp.int32, (EXPERTS, ROWS), 0)
    member = jnp.zeros((EXPERTS, ROWS), f32)
    code = jnp.zeros((EXPERTS, ROWS), f32)
    for k in range(TOPK):
        named = expert == place_of(ids_ref[k : k + 1, :])
        member = member + jnp.where(named, 1.0, 0.0)
        code = code + jnp.where(named, codes_ref[k : k + 1, :].astype(f32), 0.0)
    earlier = lax.broadcasted_iota(jnp.int32, (ROWS, ROWS), 0) < lax.broadcasted_iota(
        jnp.int32, (ROWS, ROWS), 1
    )
    rank = jnp.dot(
        member.astype(bf16), jnp.where(earlier, 1.0, 0.0).astype(bf16), preferred_element_type=f32
    )
    rows = EXPERTS * SLOTS
    own = lax.broadcasted_iota(jnp.int32, (rows, EXPERTS), 0) // SLOTS
    mine = own == lax.broadcasted_iota(jnp.int32, (rows, EXPERTS), 1)
    mine = jnp.where(mine, 1.0, 0.0).astype(bf16)
    place = jnp.dot(mine, (member * (rank + 1.0)).astype(bf16), preferred_element_type=f32)
    codes = jnp.dot(mine, code.astype(bf16), preferred_element_type=f32)
    slot = (lax.broadcasted_iota(jnp.int32, (rows, ROWS), 0) & (SLOTS - 1)) + 1
    here = place == slot.astype(f32)
    pick_ref[...] = jnp.where(here, 1.0, 0.0).astype(bf16)
    weight_ref[...] = jnp.where(here, codes, 0.0).astype(bf16)


K_STEPS = 4


def project_kernel(heads_ref, weight_ref, hidden_ref, gain_ref, pick_ref, mixed_ref, share_ref, acc):
    step = pl.program_id(0)
    per = HEADS // K_STEPS
    part = jnp.concatenate([heads_ref[i] for i in range(per)], axis=1)
    product = jnp.dot(part, weight_ref[...], preferred_element_type=f32)

    @pl.when(step == 0)
    def _():
        acc[...] = product
        for yl in range(2):
            for yh in range(2):
                for spot in range(SPOTS):
                    place = (spot // 4) * 16 + yl * 8 + (spot % 4) * 2 + yh
                    lanes = slice(spot * ROWS, (spot + 1) * ROWS)
                    picks = pick_ref[place * SLOTS : (place + 1) * SLOTS, :]
                    share_ref[yl * 2 + yh, ROWS:, lanes] = picks

    @pl.when(step > 0)
    def _():
        acc[...] += product

    @pl.when(step == K_STEPS - 1)
    def _():
        mixed = (hidden_ref[...].astype(f32) + acc[...]).astype(bf16)
        mixed_ref[...] = mixed
        wide = mixed.astype(f32)
        scale = lax.rsqrt(jnp.mean(wide * wide, axis=-1, keepdims=True) + 1e-06)
        normed = (wide * scale * gain_ref[...]).astype(bf16)
        for number in range(Y_SIZE):
            share_ref[number, 0:ROWS, :] = normed


def fill_kernel(share_ref, send_ref, rows, sems):
    copies = []
    for source in range(Y_SIZE):
        picks = [share_ref[source, ROWS:, i * ROWS : (i + 1) * ROWS] for i in range(SPOTS)]
        picked = jnp.dot(
            jnp.concatenate(picks, axis=0), share_ref[source, 0:ROWS, :], preferred_element_type=f32
        )
        rows[source] = picked.astype(bf16).reshape(SPOTS, SLOTS, D)
        copy = pltpu.make_async_copy(rows.at[source], send_ref.at[:, source], sems.at[source])
        copy.start()
        copies.append(copy)
    for copy in copies:
        copy.wait()


def expert_kernel(*refs):
    pieces = len(PIECES)
    x_any, first, second = refs[0], refs[1 : 1 + pieces], refs[1 + pieces : 1 + 2 * pieces]
    down_a, down_b, out_any, x, w_in, w_down, act, out, sems, out_sems = refs[1 + 2 * pieces :]
    blocks = x.shape[0]
    load = pltpu.make_async_copy(x_any, x, sems.at[2, 0])
    load.start()
    copies = []
    for half, parts in enumerate((first, second)):
        start = 0
        for number, (part, count) in enumerate(zip(parts, PIECES)):
            goal = w_in.at[half, pl.ds(start, count)]
            copies.append(pltpu.make_async_copy(part, goal, sems.at[half, number]))
            start += count
    for half, down in enumerate((down_a, down_b)):
        copies.append(pltpu.make_async_copy(down, w_down.at[half], sems.at[2, 1 + half]))
    for copy in copies:
        copy.start()
    load.wait()
    for half in range(2):
        for number in range(pieces):
            copies[half * pieces + number].wait()
        for block in range(blocks):
            inner = jnp.dot(x[block], w_in[half], preferred_element_type=f32)
            gate = inner[:, :HALF]
            up = pltpu.roll(inner, HALF, axis=1)[:, :HALF]
            act[half, block] = (gate / (1.0 + jnp.exp(-gate)) * up).astype(bf16)
    copies[2 * pieces].wait()
    copies[2 * pieces + 1].wait()
    sends = []
    spots = SPOTS // blocks
    for block in range(blocks):
        total = jnp.dot(act[0, block], w_down[0], preferred_element_type=f32)
        total = total + jnp.dot(act[1, block], w_down[1], preferred_element_type=f32)
        out[block] = total.astype(bf16).reshape(spots, 2, 2, SLOTS, D)
        for near in range(spots):
            spot = block * spots + near
            goal = out_any.at[spot // 4, :, spot % 4]
            send = pltpu.make_async_copy(out.at[block, near], goal, out_sems.at[spot])
            send.start()
            sends.append(send)
    for send in sends:
        send.wait()


def combine_kernel(rows_ref, weight_ref, mixed_ref, out_ref, acc, total):
    step = pl.program_id(0)
    over = (((0,), (0,)), ((), ()))
    weight = weight_ref[...]
    product = lax.dot_general(weight, rows_ref[...], over, preferred_element_type=f32)
    ones = jnp.ones((weight.shape[0], ROWS), bf16)
    count = lax.dot_general(weight, ones, over, preferred_element_type=f32)

    @pl.when(step == 0)
    def _():
        acc[...] = product
        total[...] = count

    @pl.when(step > 0)
    def _():
        acc[...] += product
        total[...] += count

    @pl.when(step == pl.num_programs(0) - 1)
    def _():
        routed = acc[...] / total[:, 0:1]
        out_ref[...] = (mixed_ref[...].astype(f32) + routed).astype(bf16)


def local(
    queries,
    keys,
    values,
    segment_ids,
    hidden_in,
    out_weight,
    norm_gain,
    expert_ids,
    gate_codes,
    w_in,
    w_down,
):
    shape = jax.ShapeDtypeStruct
    gate_up, start, moved, other = w_in[0], 0, [], []
    for count in PIECES:
        piece = lax.slice_in_dim(gate_up, start, start + count)
        moved.append(lax.ppermute(piece, AXES, moves(weight_target)))
        other.append(lax.ppermute(moved[-1], AXES, moves(core_target)))
        start += count
    moved_down = lax.ppermute(w_down[0], AXES, moves(weight_target))
    other_down = lax.ppermute(moved_down, AXES, moves(core_target))
    packed = pl.pallas_call(
        pack_kernel,
        out_shape=shape((HEADS, PACK_ROWS, HEAD_DIM), bf16),
        in_specs=[VMEM] * 4,
        out_specs=VMEM,
        compiler_params=params(60),
        name="pack",
    )(queries[0], keys[0], values[0], segment_ids)
    swapped = lax.all_to_all(packed, POSITIONS, split_axis=0, concat_axis=0, tiled=True)
    attended = pl.pallas_call(
        attend_kernel,
        out_shape=shape((HEADS, ROWS, HEAD_DIM), bf16),
        in_specs=[VMEM],
        out_specs=VMEM,
        compiler_params=params(40),
        name="attend",
    )(swapped)
    heads = lax.all_to_all(attended, POSITIONS, split_axis=0, concat_axis=0, tiled=True)
    pick, weight = pl.pallas_call(
        route_kernel,
        out_shape=(
            shape((EXPERTS * SLOTS, ROWS), bf16),
            shape((EXPERTS * SLOTS, ROWS), bf16),
        ),
        in_specs=[VMEM] * 2,
        out_specs=(VMEM, VMEM),
        compiler_params=params(60),
        name="route",
    )(expert_ids[0].T, gate_codes[0].T)
    per = HEADS // K_STEPS
    mixed, share = pl.pallas_call(
        project_kernel,
        grid=(K_STEPS,),
        out_shape=(
            shape((ROWS, D), bf16),
            shape((Y_SIZE, ROWS + SLOTS, D), bf16),
        ),
        in_specs=[
            pl.BlockSpec((per, ROWS, HEAD_DIM), lambda i: (i, 0, 0)),
            pl.BlockSpec((D // K_STEPS, D), lambda i: (i, 0)),
            pl.BlockSpec((ROWS, D), lambda i: (0, 0)),
            pl.BlockSpec((1, D), lambda i: (0, 0)),
            pl.BlockSpec((EXPERTS * SLOTS, ROWS), lambda i: (0, 0)),
        ],
        out_specs=(
            pl.BlockSpec((ROWS, D), lambda i: (0, 0)),
            pl.BlockSpec((Y_SIZE, ROWS + SLOTS, D), lambda i: (0, 0, 0)),
        ),
        scratch_shapes=[pltpu.VMEM((ROWS, D), f32)],
        compiler_params=params(53),
        name="project",
    )(heads, out_weight, hidden_in[0], norm_gain[None], pick)
    shared = lax.all_to_all(share, ("yl", "yh"), split_axis=0, concat_axis=0, tiled=True)
    send = pl.pallas_call(
        fill_kernel,
        out_shape=shape((SPOTS, Y_SIZE, SLOTS, D), bf16),
        in_specs=[VMEM],
        out_specs=pl.BlockSpec(memory_space=pl.ANY),
        scratch_shapes=[
            pltpu.VMEM((Y_SIZE, SPOTS, SLOTS, D), bf16),
            pltpu.SemaphoreType.DMA((Y_SIZE,)),
        ],
        compiler_params=params(50),
        name="fill",
    )(shared)
    arrived = lax.all_to_all(
        send.reshape(SPOTS, Y_SIZE * SLOTS, D), ("z", "x"), split_axis=0, concat_axis=0, tiled=True
    )
    blocks = EXPERTS * SLOTS // X_BLOCK
    anywhere = pl.BlockSpec(memory_space=pl.ANY)
    results = pl.pallas_call(
        expert_kernel,
        out_shape=shape((4, 2, 4, 2, SLOTS, D), bf16),
        in_specs=[anywhere] * (3 + 2 * len(PIECES)),
        out_specs=anywhere,
        scratch_shapes=[
            pltpu.VMEM((blocks, X_BLOCK, D), bf16),
            pltpu.VMEM((2, D, 2 * HALF), bf16),
            pltpu.VMEM((2, HALF, D), bf16),
            pltpu.VMEM((2, blocks, X_BLOCK, HALF), bf16),
            pltpu.VMEM((blocks, SPOTS // blocks, 2, 2, SLOTS, D), bf16),
            pltpu.SemaphoreType.DMA((3, len(PIECES))),
            pltpu.SemaphoreType.DMA((SPOTS,)),
        ],
        compiler_params=params(52),
        name="experts",
    )(arrived.reshape(blocks, X_BLOCK, D), *moved, *other, moved_down, other_down)
    returned = lax.all_to_all(
        results.reshape(EXPERTS, SLOTS, D), PLACES, split_axis=0, concat_axis=0, tiled=True
    )
    block = 256
    layer_out = pl.pallas_call(
        combine_kernel,
        grid=(EXPERTS * SLOTS // block,),
        out_shape=shape((ROWS, D), bf16),
        in_specs=[
            pl.BlockSpec((block, D), lambda i: (i, 0)),
            pl.BlockSpec((block, ROWS), lambda i: (i, 0)),
            pl.BlockSpec((ROWS, D), lambda i: (0, 0)),
        ],
        out_specs=pl.BlockSpec((ROWS, D), lambda i: (0, 0)),
        scratch_shapes=[pltpu.VMEM((ROWS, D), f32), pltpu.VMEM((ROWS, ROWS), f32)],
        compiler_params=params(12),
        name="combine",
    )(returned.reshape(EXPERTS * SLOTS, D), weight, mixed)
    return layer_out[None]


def solution(mesh):
    parts = Mesh(mesh.devices.reshape(SIZES), AXES)
    rows = P(STREAM, POSITIONS, None)
    owned = P((*POSITIONS, *STREAM), None, None)
    placed = (rows, rows, rows, P(STREAM, POSITIONS), rows, P(), P(), rows, rows, owned, owned)
    return jax.shard_map(local, mesh=parts, in_specs=placed, out_specs=rows, check_vma=False)
```

```python
import math

import jax
import jax.numpy as jnp
from jax import lax
from jax.experimental import pallas as pl
from jax.experimental.pallas import tpu as pltpu
from jax.sharding import Mesh
from jax.sharding import PartitionSpec as P

D = 2048
HEADS = 16
HEAD_DIM = 128
TOPK = 6
ROWS = 128
EXPERTS = 64
SLOTS = 16
HALF = 704
SEG_MOST = 1024
SEG_ROWS = 16
PACK_ROWS = 3 * ROWS + SEG_ROWS
Q_BLOCK = 256
X_BLOCK = 512
PIECES = (256, 384, 448, 960)
SPOTS = 16
Y_SIZE = 4
NEG_FILL = -1e30

VMEM = pl.BlockSpec(memory_space=pltpu.VMEM)
SMEM = pl.BlockSpec(memory_space=pltpu.SMEM)
f32 = jnp.float32
bf16 = jnp.bfloat16


SIZES = (4, 2, 2, 4, 2)
AXES = ("z", "yl", "c", "x", "yh")
POSITIONS = ("z", "yl", "c")
STREAM = ("x", "yh")
PLACES = ("z", "yl", "x", "yh")


def moves(target):
    pairs = []
    for number in range(math.prod(SIZES)):
        rest, spot = number, []
        for size in reversed(SIZES):
            spot.append(rest % size)
            rest //= size
        goal = 0
        for size, value in zip(SIZES, target(*reversed(spot))):
            goal = goal * size + value
        pairs.append((number, goal))
    return pairs


def weight_target(z, yl, c, x, yh):
    return (z, 1 - yl, yh, x, c)


def core_target(z, yl, c, x, yh):
    return (z, yl, 1 - c, x, yh)


def along_y(distance):
    def target(z, yl, c, x, yh):
        y = (yl + 2 * yh + distance) % Y_SIZE
        return (z, y % 2, c, x, y // 2)

    return target


def params(mib):
    return pltpu.CompilerParams(vmem_limit_bytes=mib << 20)


def pack_kernel(q_ref, k_ref, v_ref, seg_ref, out_ref):
    seg = jnp.broadcast_to(seg_ref[...].astype(f32), (SEG_ROWS, ROWS)).astype(bf16)
    for head in range(HEADS):
        lanes = slice(head * HEAD_DIM, (head + 1) * HEAD_DIM)
        out_ref[head, 0:ROWS, :] = q_ref[:, lanes]
        out_ref[head, ROWS : 2 * ROWS, :] = k_ref[:, lanes]
        out_ref[head, 2 * ROWS : 3 * ROWS, :] = v_ref[:, lanes]
        out_ref[head, 3 * ROWS :, :] = seg


def attend_kernel(x_ref, out_ref):
    blocks = x_ref.shape[0]
    seg = x_ref[:, 3 * ROWS :, :].astype(f32)
    first = (jnp.sum(jnp.where(seg < 0.5, 1.0, 0.0)) * (1.0 / SEG_ROWS)).astype(jnp.int32)
    second = (jnp.sum(jnp.where(seg < 1.5, 1.0, 0.0)) * (1.0 / SEG_ROWS)).astype(jnp.int32)
    per = Q_BLOCK // ROWS
    for block in range(blocks // per):
        start = block * per
        low = max(0, start - SEG_MOST // ROWS)
        high = start + per
        width = (high - low) * ROWS
        query = x_ref[start:high, 0:ROWS, :].reshape(Q_BLOCK, HEAD_DIM)
        key = x_ref[low:high, ROWS : 2 * ROWS, :].reshape(width, HEAD_DIM)
        value = x_ref[low:high, 2 * ROWS : 3 * ROWS, :].reshape(width, HEAD_DIM)
        scores = lax.dot_general(
            query, key, (((1,), (1,)), ((), ())), preferred_element_type=f32
        ) * HEAD_DIM ** (-0.5)
        row = start * ROWS + lax.broadcasted_iota(jnp.int32, (Q_BLOCK, 1), 0)
        column = low * ROWS + lax.broadcasted_iota(jnp.int32, (Q_BLOCK, width), 1)
        begin = jnp.where(row < first, 0, jnp.where(row < second, first, second))
        allowed = (column <= row) & (column >= begin)
        scores = jnp.where(allowed, scores, NEG_FILL)
        top = jnp.max(scores, axis=-1, keepdims=True)
        probs = jnp.exp(scores - top)
        total = jnp.sum(probs, axis=-1, keepdims=True)
        mixed = jnp.dot(probs.astype(bf16), value, preferred_element_type=f32)
        out_ref[start:high] = (mixed / total).astype(bf16).reshape(per, ROWS, HEAD_DIM)


def place_of(expert):
    return (expert & 48) | (8 - (expert & 8)) | ((expert & 3) << 1) | ((expert >> 2) & 1)


def reach_of(expert, y):
    distance = (1 - ((expert >> 3) & 1) + ((expert >> 1) & 2) - y) & 3
    return (distance << 4) | ((expert >> 2) & 12) | (expert & 3)


def route_kernel(y_ref, ids_ref, codes_ref, pick_ref, weight_ref):
    number = lax.broadcasted_iota(jnp.int32, (EXPERTS, ROWS), 0)
    earlier = lax.broadcasted_iota(jnp.int32, (ROWS, ROWS), 0) < lax.broadcasted_iota(
        jnp.int32, (ROWS, ROWS), 1
    )
    earlier = jnp.where(earlier, 1.0, 0.0).astype(bf16)
    rows = EXPERTS * SLOTS
    own = lax.broadcasted_iota(jnp.int32, (rows, EXPERTS), 0) // SLOTS
    mine = own == lax.broadcasted_iota(jnp.int32, (rows, EXPERTS), 1)
    mine = jnp.where(mine, 1.0, 0.0).astype(bf16)
    slot = (lax.broadcasted_iota(jnp.int32, (rows, ROWS), 0) & (SLOTS - 1)) + 1
    ids = ids_ref[...]

    def ordered(names):
        member = jnp.zeros((EXPERTS, ROWS), f32)
        code = jnp.zeros((EXPERTS, ROWS), f32)
        for k in range(TOPK):
            named = number == names[k : k + 1, :]
            member = member + jnp.where(named, 1.0, 0.0)
            code = code + jnp.where(named, codes_ref[k : k + 1, :].astype(f32), 0.0)
        rank = jnp.dot(member.astype(bf16), earlier, preferred_element_type=f32)
        place = jnp.dot(mine, (member * (rank + 1.0)).astype(bf16), preferred_element_type=f32)
        return place == slot.astype(f32), code

    here, _ = ordered(reach_of(ids, y_ref[0]))
    pick_ref[...] = jnp.where(here, 1.0, 0.0).astype(bf16)
    here, code = ordered(place_of(ids))
    codes = jnp.dot(mine, code.astype(bf16), preferred_element_type=f32)
    weight_ref[...] = jnp.where(here, codes, 0.0).astype(bf16)


K_STEPS = 4


def project_kernel(heads_ref, weight_ref, hidden_ref, gain_ref, pick_ref, mixed_ref, *rest):
    shares, own_ref, acc = rest[:3], rest[3], rest[4]
    step = pl.program_id(0)
    per = HEADS // K_STEPS
    part = jnp.concatenate([heads_ref[i] for i in range(per)], axis=1)
    product = jnp.dot(part, weight_ref[...], preferred_element_type=f32)

    @pl.when(step == 0)
    def _():
        acc[...] = product
        for distance in range(1, Y_SIZE):
            for spot in range(SPOTS):
                lanes = slice(spot * ROWS, (spot + 1) * ROWS)
                first = (distance * SPOTS + spot) * SLOTS
                shares[distance - 1][ROWS:, lanes] = pick_ref[first : first + SLOTS, :]

    @pl.when(step > 0)
    def _():
        acc[...] += product

    @pl.when(step == K_STEPS - 1)
    def _():
        mixed = (hidden_ref[...].astype(f32) + acc[...]).astype(bf16)
        mixed_ref[...] = mixed
        wide = mixed.astype(f32)
        scale = lax.rsqrt(jnp.mean(wide * wide, axis=-1, keepdims=True) + 1e-06)
        normed = (wide * scale * gain_ref[...]).astype(bf16)
        for share_ref in shares:
            share_ref[0:ROWS, :] = normed
        picked = jnp.dot(pick_ref[: SPOTS * SLOTS, :], normed, preferred_element_type=f32)
        own_ref[...] = picked.astype(bf16).reshape(SPOTS, SLOTS, D)


def fill_kernel(near_ref, far_ref, back_ref, send_ref, rows, sems):
    copies = []
    for source, share_ref in enumerate((near_ref, back_ref, far_ref)):
        picks = [share_ref[ROWS:, i * ROWS : (i + 1) * ROWS] for i in range(SPOTS)]
        picked = jnp.dot(
            jnp.concatenate(picks, axis=0), share_ref[0:ROWS, :], preferred_element_type=f32
        )
        rows[source] = picked.astype(bf16).reshape(SPOTS, SLOTS, D)
        copy = pltpu.make_async_copy(rows.at[source], send_ref.at[:, source], sems.at[source])
        copy.start()
        copies.append(copy)
    for copy in copies:
        copy.wait()


def origin(unit):
    if unit < SPOTS:
        return unit, 0
    return (unit - SPOTS) // 3, (3, 1, 2)[(unit - SPOTS) % 3]


def expert_kernel(*refs):
    pieces = len(PIECES)
    y_ref, own_any, x_any, refs = refs[0], refs[1], refs[2], refs[3:]
    first, second = refs[:pieces], refs[pieces : 2 * pieces]
    down_a, down_b, out_any, x, w_in, w_down, act, out, sems, out_sems = refs[2 * pieces :]
    y = y_ref[0]
    blocks = x.shape[0] // X_BLOCK
    own_rows = SPOTS * SLOTS
    loads = [
        pltpu.make_async_copy(own_any, x.at[pl.ds(0, own_rows)], sems.at[2, 0]),
        pltpu.make_async_copy(x_any, x.at[pl.ds(own_rows, 3 * own_rows)], sems.at[2, 3]),
    ]
    for load in loads:
        load.start()
    copies = []
    for half, parts in enumerate((first, second)):
        start = 0
        for number, (part, count) in enumerate(zip(parts, PIECES)):
            goal = w_in.at[half, pl.ds(start, count)]
            copies.append(pltpu.make_async_copy(part, goal, sems.at[half, number]))
            start += count
    for half, down in enumerate((down_a, down_b)):
        copies.append(pltpu.make_async_copy(down, w_down.at[half], sems.at[2, 1 + half]))
    for copy in copies:
        copy.start()
    for load in loads:
        load.wait()
    for half in range(2):
        for number in range(pieces):
            copies[half * pieces + number].wait()
        for block in range(blocks):
            rows = x[block * X_BLOCK : (block + 1) * X_BLOCK, :]
            inner = jnp.dot(rows, w_in[half], preferred_element_type=f32)
            gate = inner[:, :HALF]
            up = pltpu.roll(inner, HALF, axis=1)[:, :HALF]
            act[half, block] = (gate / (1.0 + jnp.exp(-gate)) * up).astype(bf16)
    copies[2 * pieces].wait()
    copies[2 * pieces + 1].wait()
    sends = []
    units = X_BLOCK // SLOTS
    for block in range(blocks):
        total = jnp.dot(act[0, block], w_down[0], preferred_element_type=f32)
        total = total + jnp.dot(act[1, block], w_down[1], preferred_element_type=f32)
        out[block] = total.astype(bf16).reshape(units, SLOTS, D)
        for near in range(units):
            unit = block * units + near
            spot, ahead = origin(unit)
            from_y = (y + ahead) & 3
            goal = out_any.at[spot // 4, from_y & 1, spot % 4, from_y >> 1]
            send = pltpu.make_async_copy(out.at[block, near], goal, out_sems.at[unit])
            send.start()
            sends.append(send)
    for send in sends:
        send.wait()


def combine_kernel(rows_ref, weight_ref, mixed_ref, out_ref, acc, total):
    step = pl.program_id(0)
    over = (((0,), (0,)), ((), ()))
    weight = weight_ref[...]
    product = lax.dot_general(weight, rows_ref[...], over, preferred_element_type=f32)
    ones = jnp.ones((weight.shape[0], ROWS), bf16)
    count = lax.dot_general(weight, ones, over, preferred_element_type=f32)

    @pl.when(step == 0)
    def _():
        acc[...] = product
        total[...] = count

    @pl.when(step > 0)
    def _():
        acc[...] += product
        total[...] += count

    @pl.when(step == pl.num_programs(0) - 1)
    def _():
        routed = acc[...] / total[:, 0:1]
        out_ref[...] = (mixed_ref[...].astype(f32) + routed).astype(bf16)


def local(
    queries,
    keys,
    values,
    segment_ids,
    hidden_in,
    out_weight,
    norm_gain,
    expert_ids,
    gate_codes,
    w_in,
    w_down,
):
    shape = jax.ShapeDtypeStruct
    y = (lax.axis_index("yl") + 2 * lax.axis_index("yh")).astype(jnp.int32)[None]
    gate_up, start, moved, other = w_in[0], 0, [], []
    for count in PIECES:
        piece = lax.slice_in_dim(gate_up, start, start + count)
        moved.append(lax.ppermute(piece, AXES, moves(weight_target)))
        other.append(lax.ppermute(moved[-1], AXES, moves(core_target)))
        start += count
    moved_down = lax.ppermute(w_down[0], AXES, moves(weight_target))
    other_down = lax.ppermute(moved_down, AXES, moves(core_target))
    packed = pl.pallas_call(
        pack_kernel,
        out_shape=shape((HEADS, PACK_ROWS, HEAD_DIM), bf16),
        in_specs=[VMEM] * 4,
        out_specs=VMEM,
        compiler_params=params(60),
        name="pack",
    )(queries[0], keys[0], values[0], segment_ids)
    swapped = lax.all_to_all(packed, POSITIONS, split_axis=0, concat_axis=0, tiled=True)
    attended = pl.pallas_call(
        attend_kernel,
        out_shape=shape((HEADS, ROWS, HEAD_DIM), bf16),
        in_specs=[VMEM],
        out_specs=VMEM,
        compiler_params=params(40),
        name="attend",
    )(swapped)
    heads = lax.all_to_all(attended, POSITIONS, split_axis=0, concat_axis=0, tiled=True)
    pick, weight = pl.pallas_call(
        route_kernel,
        out_shape=(
            shape((EXPERTS * SLOTS, ROWS), bf16),
            shape((EXPERTS * SLOTS, ROWS), bf16),
        ),
        in_specs=[SMEM, VMEM, VMEM],
        out_specs=(VMEM, VMEM),
        compiler_params=params(60),
        name="route",
    )(y, expert_ids[0].T, gate_codes[0].T)
    per = HEADS // K_STEPS
    share_shape = (ROWS + SLOTS, D)
    mixed, *shares, own = pl.pallas_call(
        project_kernel,
        grid=(K_STEPS,),
        out_shape=(
            shape((ROWS, D), bf16),
            shape(share_shape, bf16),
            shape(share_shape, bf16),
            shape(share_shape, bf16),
            shape((SPOTS, SLOTS, D), bf16),
        ),
        in_specs=[
            pl.BlockSpec((per, ROWS, HEAD_DIM), lambda i: (i, 0, 0)),
            pl.BlockSpec((D // K_STEPS, D), lambda i: (i, 0)),
            pl.BlockSpec((ROWS, D), lambda i: (0, 0)),
            pl.BlockSpec((1, D), lambda i: (0, 0)),
            pl.BlockSpec((EXPERTS * SLOTS, ROWS), lambda i: (0, 0)),
        ],
        out_specs=(
            pl.BlockSpec((ROWS, D), lambda i: (0, 0)),
            pl.BlockSpec(share_shape, lambda i: (0, 0)),
            pl.BlockSpec(share_shape, lambda i: (0, 0)),
            pl.BlockSpec(share_shape, lambda i: (0, 0)),
            pl.BlockSpec((SPOTS, SLOTS, D), lambda i: (0, 0, 0)),
        ),
        scratch_shapes=[pltpu.VMEM((ROWS, D), f32)],
        compiler_params=params(53),
        name="project",
    )(heads, out_weight, hidden_in[0], norm_gain[None], pick)
    arriving = []
    for distance, share in enumerate(shares, 1):
        arriving.append(lax.ppermute(share, AXES, moves(along_y(distance))))
    arrived_own = lax.all_to_all(own, ("z", "x"), split_axis=0, concat_axis=0, tiled=True)
    near, far, back = arriving
    send = pl.pallas_call(
        fill_kernel,
        out_shape=shape((SPOTS, 3, SLOTS, D), bf16),
        in_specs=[VMEM] * 3,
        out_specs=pl.BlockSpec(memory_space=pl.ANY),
        scratch_shapes=[
            pltpu.VMEM((3, SPOTS, SLOTS, D), bf16),
            pltpu.SemaphoreType.DMA((3,)),
        ],
        compiler_params=params(50),
        name="fill",
    )(near, far, back)
    arrived = lax.all_to_all(
        send.reshape(SPOTS, 3 * SLOTS, D), ("z", "x"), split_axis=0, concat_axis=0, tiled=True
    )
    blocks = EXPERTS * SLOTS // X_BLOCK
    anywhere = pl.BlockSpec(memory_space=pl.ANY)
    results = pl.pallas_call(
        expert_kernel,
        out_shape=shape((4, 2, 4, 2, SLOTS, D), bf16),
        in_specs=[SMEM] + [anywhere] * (4 + 2 * len(PIECES)),
        out_specs=anywhere,
        scratch_shapes=[
            pltpu.VMEM((EXPERTS * SLOTS, D), bf16),
            pltpu.VMEM((2, D, 2 * HALF), bf16),
            pltpu.VMEM((2, HALF, D), bf16),
            pltpu.VMEM((2, blocks, X_BLOCK, HALF), bf16),
            pltpu.VMEM((blocks, X_BLOCK // SLOTS, SLOTS, D), bf16),
            pltpu.SemaphoreType.DMA((3, len(PIECES))),
            pltpu.SemaphoreType.DMA((EXPERTS,)),
        ],
        compiler_params=params(52),
        name="experts",
    )(
        y,
        arrived_own.reshape(SPOTS * SLOTS, D),
        arrived.reshape(3 * SPOTS * SLOTS, D),
        *moved,
        *other,
        moved_down,
        other_down,
    )
    returned = lax.all_to_all(
        results.reshape(EXPERTS, SLOTS, D), PLACES, split_axis=0, concat_axis=0, tiled=True
    )
    block = 256
    layer_out = pl.pallas_call(
        combine_kernel,
        grid=(EXPERTS * SLOTS // block,),
        out_shape=shape((ROWS, D), bf16),
        in_specs=[
            pl.BlockSpec((block, D), lambda i: (i, 0)),
            pl.BlockSpec((block, ROWS), lambda i: (i, 0)),
            pl.BlockSpec((ROWS, D), lambda i: (0, 0)),
        ],
        out_specs=pl.BlockSpec((ROWS, D), lambda i: (0, 0)),
        scratch_shapes=[pltpu.VMEM((ROWS, D), f32), pltpu.VMEM((ROWS, ROWS), f32)],
        compiler_params=params(12),
        name="combine",
    )(returned.reshape(EXPERTS * SLOTS, D), weight, mixed)
    return layer_out[None]


def solution(mesh):
    parts = Mesh(mesh.devices.reshape(SIZES), AXES)
    rows = P(STREAM, POSITIONS, None)
    owned = P((*POSITIONS, *STREAM), None, None)
    placed = (rows, rows, rows, P(STREAM, POSITIONS), rows, P(), P(), rows, rows, owned, owned)
    return jax.shard_map(local, mesh=parts, in_specs=placed, out_specs=rows, check_vma=False)
```

```python
import math

import jax
import jax.numpy as jnp
from jax import lax
from jax.experimental import pallas as pl
from jax.experimental.pallas import tpu as pltpu
from jax.sharding import Mesh
from jax.sharding import PartitionSpec as P

D = 2048
HEADS = 16
HEAD_DIM = 128
TOPK = 6
ROWS = 128
EXPERTS = 64
SLOTS = 16
HALF = 704
SEG_MOST = 1024
SEG_ROWS = 16
PACK_ROWS = 3 * ROWS + SEG_ROWS
Q_BLOCK = 256
X_BLOCK = 256
PIECES = (256, 384, 448, 960)
SPOTS = 16
Y_SIZE = 4
NEG_FILL = -1e30

VMEM = pl.BlockSpec(memory_space=pltpu.VMEM)
SMEM = pl.BlockSpec(memory_space=pltpu.SMEM)
f32 = jnp.float32
bf16 = jnp.bfloat16


SIZES = (4, 2, 2, 4, 2)
AXES = ("z", "yl", "c", "x", "yh")
POSITIONS = ("z", "yl", "c")
STREAM = ("x", "yh")
PLACES = ("z", "yl", "x", "yh")


def moves(target):
    pairs = []
    for number in range(math.prod(SIZES)):
        rest, spot = number, []
        for size in reversed(SIZES):
            spot.append(rest % size)
            rest //= size
        goal = 0
        for size, value in zip(SIZES, target(*reversed(spot))):
            goal = goal * size + value
        pairs.append((number, goal))
    return pairs


def weight_target(z, yl, c, x, yh):
    return (z, 1 - yl, yh, x, c)


def core_target(z, yl, c, x, yh):
    return (z, yl, 1 - c, x, yh)


def along_y(distance):
    def target(z, yl, c, x, yh):
        y = (yl + 2 * yh + distance) % Y_SIZE
        return (z, y % 2, c, x, y // 2)

    return target


def params(mib):
    return pltpu.CompilerParams(vmem_limit_bytes=mib << 20)


def pack_kernel(q_ref, k_ref, v_ref, seg_ref, out_ref):
    seg = jnp.broadcast_to(seg_ref[...].astype(f32), (SEG_ROWS, ROWS)).astype(bf16)
    for head in range(HEADS):
        lanes = slice(head * HEAD_DIM, (head + 1) * HEAD_DIM)
        out_ref[head, 0:ROWS, :] = q_ref[:, lanes]
        out_ref[head, ROWS : 2 * ROWS, :] = k_ref[:, lanes]
        out_ref[head, 2 * ROWS : 3 * ROWS, :] = v_ref[:, lanes]
        out_ref[head, 3 * ROWS :, :] = seg


def attend_kernel(x_ref, out_ref):
    blocks = x_ref.shape[0]
    seg = x_ref[:, 3 * ROWS :, :].astype(f32)
    first = (jnp.sum(jnp.where(seg < 0.5, 1.0, 0.0)) * (1.0 / SEG_ROWS)).astype(jnp.int32)
    second = (jnp.sum(jnp.where(seg < 1.5, 1.0, 0.0)) * (1.0 / SEG_ROWS)).astype(jnp.int32)
    per = Q_BLOCK // ROWS
    for block in range(blocks // per):
        start = block * per
        low = max(0, start - SEG_MOST // ROWS)
        high = start + per
        width = (high - low) * ROWS
        query = x_ref[start:high, 0:ROWS, :].reshape(Q_BLOCK, HEAD_DIM)
        key = x_ref[low:high, ROWS : 2 * ROWS, :].reshape(width, HEAD_DIM)
        value = x_ref[low:high, 2 * ROWS : 3 * ROWS, :].reshape(width, HEAD_DIM)
        scores = lax.dot_general(
            query, key, (((1,), (1,)), ((), ())), preferred_element_type=f32
        ) * HEAD_DIM ** (-0.5)
        row = start * ROWS + lax.broadcasted_iota(jnp.int32, (Q_BLOCK, 1), 0)
        column = low * ROWS + lax.broadcasted_iota(jnp.int32, (Q_BLOCK, width), 1)
        begin = jnp.where(row < first, 0, jnp.where(row < second, first, second))
        allowed = (column <= row) & (column >= begin)
        scores = jnp.where(allowed, scores, NEG_FILL)
        top = jnp.max(scores, axis=-1, keepdims=True)
        probs = jnp.exp(scores - top)
        total = jnp.sum(probs, axis=-1, keepdims=True)
        mixed = jnp.dot(probs.astype(bf16), value, preferred_element_type=f32)
        out_ref[start:high] = (mixed / total).astype(bf16).reshape(per, ROWS, HEAD_DIM)


def place_of(expert):
    return (expert & 48) | (8 - (expert & 8)) | ((expert & 3) << 1) | ((expert >> 2) & 1)


def reach_of(expert, y):
    distance = (1 - ((expert >> 3) & 1) + ((expert >> 1) & 2) - y) & 3
    return (distance << 4) | ((expert >> 2) & 12) | (expert & 3)


def route_kernel(y_ref, ids_ref, codes_ref, pick_ref, weight_ref):
    number = lax.broadcasted_iota(jnp.int32, (EXPERTS, ROWS), 0)
    earlier = lax.broadcasted_iota(jnp.int32, (ROWS, ROWS), 0) < lax.broadcasted_iota(
        jnp.int32, (ROWS, ROWS), 1
    )
    earlier = jnp.where(earlier, 1.0, 0.0).astype(bf16)
    rows = EXPERTS * SLOTS
    own = lax.broadcasted_iota(jnp.int32, (rows, EXPERTS), 0) // SLOTS
    mine = own == lax.broadcasted_iota(jnp.int32, (rows, EXPERTS), 1)
    mine = jnp.where(mine, 1.0, 0.0).astype(bf16)
    slot = (lax.broadcasted_iota(jnp.int32, (rows, ROWS), 0) & (SLOTS - 1)) + 1
    ids = ids_ref[...]

    def ordered(names):
        member = jnp.zeros((EXPERTS, ROWS), f32)
        code = jnp.zeros((EXPERTS, ROWS), f32)
        for k in range(TOPK):
            named = number == names[k : k + 1, :]
            member = member + jnp.where(named, 1.0, 0.0)
            code = code + jnp.where(named, codes_ref[k : k + 1, :].astype(f32), 0.0)
        rank = jnp.dot(member.astype(bf16), earlier, preferred_element_type=f32)
        place = jnp.dot(mine, (member * (rank + 1.0)).astype(bf16), preferred_element_type=f32)
        return place == slot.astype(f32), code

    here, _ = ordered(reach_of(ids, y_ref[0]))
    pick_ref[...] = jnp.where(here, 1.0, 0.0).astype(bf16)
    here, code = ordered(place_of(ids))
    codes = jnp.dot(mine, code.astype(bf16), preferred_element_type=f32)
    weight_ref[...] = jnp.where(here, codes, 0.0).astype(bf16)


K_STEPS = 4


def project_kernel(heads_ref, weight_ref, hidden_ref, gain_ref, pick_ref, mixed_ref, *rest):
    shares, own_ref, acc = rest[:3], rest[3], rest[4]
    step = pl.program_id(0)
    per = HEADS // K_STEPS
    part = jnp.concatenate([heads_ref[i] for i in range(per)], axis=1)
    product = jnp.dot(part, weight_ref[...], preferred_element_type=f32)

    @pl.when(step == 0)
    def _():
        acc[...] = product
        for distance in range(1, Y_SIZE):
            for spot in range(SPOTS):
                lanes = slice(spot * ROWS, (spot + 1) * ROWS)
                first = (distance * SPOTS + spot) * SLOTS
                shares[distance - 1][ROWS:, lanes] = pick_ref[first : first + SLOTS, :]

    @pl.when(step > 0)
    def _():
        acc[...] += product

    @pl.when(step == K_STEPS - 1)
    def _():
        mixed = (hidden_ref[...].astype(f32) + acc[...]).astype(bf16)
        mixed_ref[...] = mixed
        wide = mixed.astype(f32)
        scale = lax.rsqrt(jnp.mean(wide * wide, axis=-1, keepdims=True) + 1e-06)
        normed = (wide * scale * gain_ref[...]).astype(bf16)
        for share_ref in shares:
            share_ref[0:ROWS, :] = normed
        picked = jnp.dot(pick_ref[: SPOTS * SLOTS, :], normed, preferred_element_type=f32)
        own_ref[...] = picked.astype(bf16).reshape(SPOTS, SLOTS, D)


def fill_kernel(near_ref, far_ref, back_ref, send_ref, rows, sems):
    copies = []
    for source, share_ref in enumerate((near_ref, back_ref, far_ref)):
        picks = [share_ref[ROWS:, i * ROWS : (i + 1) * ROWS] for i in range(SPOTS)]
        picked = jnp.dot(
            jnp.concatenate(picks, axis=0), share_ref[0:ROWS, :], preferred_element_type=f32
        )
        rows[source] = picked.astype(bf16).reshape(SPOTS, SLOTS, D)
        copy = pltpu.make_async_copy(rows.at[source], send_ref.at[:, source], sems.at[source])
        copy.start()
        copies.append(copy)
    for copy in copies:
        copy.wait()


def origin(unit):
    if unit < SPOTS:
        return unit, 0
    return (unit - SPOTS) // 3, (3, 1, 2)[(unit - SPOTS) % 3]


def inner_kernel(own_ref, rest_ref, *refs):
    pieces = len(PIECES)
    parts, (act, w_in, sems) = refs[:pieces], refs[pieces:]
    copies, start = [], 0
    for number, (part, count) in enumerate(zip(parts, PIECES)):
        goal = w_in.at[pl.ds(start, count)]
        copies.append(pltpu.make_async_copy(part, goal, sems.at[number]))
        start += count
    for copy in copies:
        copy.start()
    for copy in copies:
        copy.wait()
    for block in range(EXPERTS * SLOTS // X_BLOCK):
        first = (block - 1) * X_BLOCK
        rows = own_ref[...] if block == 0 else rest_ref[first : first + X_BLOCK, :]
        inner = jnp.dot(rows, w_in[...], preferred_element_type=f32)
        gate = inner[:, :HALF]
        up = pltpu.roll(inner, HALF, axis=1)[:, :HALF]
        act[block * X_BLOCK : (block + 1) * X_BLOCK, :] = (
            gate / (1.0 + jnp.exp(-gate)) * up
        ).astype(bf16)


def down_kernel(y_ref, act_a, act_b, down_a, down_b, out_any, out, out_sems):
    y = y_ref[0]
    sends = []
    units = X_BLOCK // SLOTS
    for block in range(EXPERTS * SLOTS // X_BLOCK):
        span = slice(block * X_BLOCK, (block + 1) * X_BLOCK)
        total = jnp.dot(act_a[span, :], down_a[...], preferred_element_type=f32)
        total = total + jnp.dot(act_b[span, :], down_b[...], preferred_element_type=f32)
        out[block] = total.astype(bf16).reshape(units, SLOTS, D)
        for near in range(units):
            unit = block * units + near
            spot, ahead = origin(unit)
            from_y = (y + ahead) & 3
            goal = out_any.at[spot // 4, from_y & 1, spot % 4, from_y >> 1]
            send = pltpu.make_async_copy(out.at[block, near], goal, out_sems.at[unit])
            send.start()
            sends.append(send)
    for send in sends:
        send.wait()


def combine_kernel(rows_ref, weight_ref, mixed_ref, out_ref, acc, total):
    step = pl.program_id(0)
    over = (((0,), (0,)), ((), ()))
    weight = weight_ref[...]
    product = lax.dot_general(weight, rows_ref[...], over, preferred_element_type=f32)
    ones = jnp.ones((weight.shape[0], ROWS), bf16)
    count = lax.dot_general(weight, ones, over, preferred_element_type=f32)

    @pl.when(step == 0)
    def _():
        acc[...] = product
        total[...] = count

    @pl.when(step > 0)
    def _():
        acc[...] += product
        total[...] += count

    @pl.when(step == pl.num_programs(0) - 1)
    def _():
        routed = acc[...] / total[:, 0:1]
        out_ref[...] = (mixed_ref[...].astype(f32) + routed).astype(bf16)


def local(
    queries,
    keys,
    values,
    segment_ids,
    hidden_in,
    out_weight,
    norm_gain,
    expert_ids,
    gate_codes,
    w_in,
    w_down,
):
    shape = jax.ShapeDtypeStruct
    y = (lax.axis_index("yl") + 2 * lax.axis_index("yh")).astype(jnp.int32)[None]
    gate_up, start, moved, other = w_in[0], 0, [], []
    for count in PIECES:
        piece = lax.slice_in_dim(gate_up, start, start + count)
        moved.append(lax.ppermute(piece, AXES, moves(weight_target)))
        other.append(lax.ppermute(moved[-1], AXES, moves(core_target)))
        start += count
    moved_down = lax.ppermute(w_down[0], AXES, moves(weight_target))
    other_down = lax.ppermute(moved_down, AXES, moves(core_target))
    packed = pl.pallas_call(
        pack_kernel,
        out_shape=shape((HEADS, PACK_ROWS, HEAD_DIM), bf16),
        in_specs=[VMEM] * 4,
        out_specs=VMEM,
        compiler_params=params(60),
        name="pack",
    )(queries[0], keys[0], values[0], segment_ids)
    swapped = lax.all_to_all(packed, POSITIONS, split_axis=0, concat_axis=0, tiled=True)
    attended = pl.pallas_call(
        attend_kernel,
        out_shape=shape((HEADS, ROWS, HEAD_DIM), bf16),
        in_specs=[VMEM],
        out_specs=VMEM,
        compiler_params=params(40),
        name="attend",
    )(swapped)
    heads = lax.all_to_all(attended, POSITIONS, split_axis=0, concat_axis=0, tiled=True)
    pick, weight = pl.pallas_call(
        route_kernel,
        out_shape=(
            shape((EXPERTS * SLOTS, ROWS), bf16),
            shape((EXPERTS * SLOTS, ROWS), bf16),
        ),
        in_specs=[SMEM, VMEM, VMEM],
        out_specs=(VMEM, VMEM),
        compiler_params=params(60),
        name="route",
    )(y, expert_ids[0].T, gate_codes[0].T)
    per = HEADS // K_STEPS
    share_shape = (ROWS + SLOTS, D)
    mixed, *shares, own = pl.pallas_call(
        project_kernel,
        grid=(K_STEPS,),
        out_shape=(
            shape((ROWS, D), bf16),
            shape(share_shape, bf16),
            shape(share_shape, bf16),
            shape(share_shape, bf16),
            shape((SPOTS, SLOTS, D), bf16),
        ),
        in_specs=[
            pl.BlockSpec((per, ROWS, HEAD_DIM), lambda i: (i, 0, 0)),
            pl.BlockSpec((D // K_STEPS, D), lambda i: (i, 0)),
            pl.BlockSpec((ROWS, D), lambda i: (0, 0)),
            pl.BlockSpec((1, D), lambda i: (0, 0)),
            pl.BlockSpec((EXPERTS * SLOTS, ROWS), lambda i: (0, 0)),
        ],
        out_specs=(
            pl.BlockSpec((ROWS, D), lambda i: (0, 0)),
            pl.BlockSpec(share_shape, lambda i: (0, 0)),
            pl.BlockSpec(share_shape, lambda i: (0, 0)),
            pl.BlockSpec(share_shape, lambda i: (0, 0)),
            pl.BlockSpec((SPOTS, SLOTS, D), lambda i: (0, 0, 0)),
        ),
        scratch_shapes=[pltpu.VMEM((ROWS, D), f32)],
        compiler_params=params(53),
        name="project",
    )(heads, out_weight, hidden_in[0], norm_gain[None], pick)
    arriving = []
    for distance, share in enumerate(shares, 1):
        arriving.append(lax.ppermute(share, AXES, moves(along_y(distance))))
    arrived_own = lax.all_to_all(own, ("z", "x"), split_axis=0, concat_axis=0, tiled=True)
    near, far, back = arriving
    send = pl.pallas_call(
        fill_kernel,
        out_shape=shape((SPOTS, 3, SLOTS, D), bf16),
        in_specs=[VMEM] * 3,
        out_specs=pl.BlockSpec(memory_space=pl.ANY),
        scratch_shapes=[
            pltpu.VMEM((3, SPOTS, SLOTS, D), bf16),
            pltpu.SemaphoreType.DMA((3,)),
        ],
        compiler_params=params(50),
        name="fill",
    )(near, far, back)
    arrived = lax.all_to_all(
        send.reshape(SPOTS, 3 * SLOTS, D), ("z", "x"), split_axis=0, concat_axis=0, tiled=True
    )
    blocks = EXPERTS * SLOTS // X_BLOCK
    anywhere = pl.BlockSpec(memory_space=pl.ANY)

    def inner(parts):
        return pl.pallas_call(
            inner_kernel,
            out_shape=shape((EXPERTS * SLOTS, HALF), bf16),
            in_specs=[VMEM, VMEM] + [anywhere] * len(PIECES),
            out_specs=VMEM,
            scratch_shapes=[
                pltpu.VMEM((D, 2 * HALF), bf16),
                pltpu.SemaphoreType.DMA((len(PIECES),)),
            ],
            compiler_params=params(32),
        )(
            arrived_own.reshape(SPOTS * SLOTS, D),
            arrived.reshape(3 * SPOTS * SLOTS, D),
            *parts,
        )

    act_a = inner(moved)
    act_b = inner(other)
    results = pl.pallas_call(
        down_kernel,
        out_shape=shape((4, 2, 4, 2, SLOTS, D), bf16),
        in_specs=[SMEM] + [VMEM] * 4,
        out_specs=anywhere,
        scratch_shapes=[
            pltpu.VMEM((blocks, X_BLOCK // SLOTS, SLOTS, D), bf16),
            pltpu.SemaphoreType.DMA((EXPERTS,)),
        ],
        compiler_params=params(32),
        name="down",
    )(y, act_a, act_b, moved_down, other_down)
    returned = lax.all_to_all(
        results.reshape(EXPERTS, SLOTS, D), PLACES, split_axis=0, concat_axis=0, tiled=True
    )
    block = 256
    layer_out = pl.pallas_call(
        combine_kernel,
        grid=(EXPERTS * SLOTS // block,),
        out_shape=shape((ROWS, D), bf16),
        in_specs=[
            pl.BlockSpec((block, D), lambda i: (i, 0)),
            pl.BlockSpec((block, ROWS), lambda i: (i, 0)),
            pl.BlockSpec((ROWS, D), lambda i: (0, 0)),
        ],
        out_specs=pl.BlockSpec((ROWS, D), lambda i: (0, 0)),
        scratch_shapes=[pltpu.VMEM((ROWS, D), f32), pltpu.VMEM((ROWS, ROWS), f32)],
        compiler_params=params(12),
        name="combine",
    )(returned.reshape(EXPERTS * SLOTS, D), weight, mixed)
    return layer_out[None]


def solution(mesh):
    parts = Mesh(mesh.devices.reshape(SIZES), AXES)
    rows = P(STREAM, POSITIONS, None)
    owned = P((*POSITIONS, *STREAM), None, None)
    placed = (rows, rows, rows, P(STREAM, POSITIONS), rows, P(), P(), rows, rows, owned, owned)
    return jax.shard_map(local, mesh=parts, in_specs=placed, out_specs=rows, check_vma=False)
```

```python
import math

import jax
import jax.numpy as jnp
from jax import lax
from jax.experimental import pallas as pl
from jax.experimental.pallas import tpu as pltpu
from jax.sharding import Mesh
from jax.sharding import PartitionSpec as P

D = 2048
HEADS = 16
HEAD_DIM = 128
TOPK = 6
ROWS = 128
EXPERTS = 64
SLOTS = 16
HALF = 704
SEG_MOST = 1024
SEG_ROWS = 16
PACK_ROWS = 3 * ROWS + SEG_ROWS
Q_BLOCK = 256
X_BLOCK = 256
PIECES = (256, 384, 448, 960)
SPOTS = 16
Y_SIZE = 4
NEG_FILL = -1e30

VMEM = pl.BlockSpec(memory_space=pltpu.VMEM)
SMEM = pl.BlockSpec(memory_space=pltpu.SMEM)
f32 = jnp.float32
bf16 = jnp.bfloat16


SIZES = (4, 2, 2, 4, 2)
AXES = ("z", "yl", "c", "x", "yh")
POSITIONS = ("z", "yl", "c")
STREAM = ("x", "yh")
PLACES = ("z", "yl", "x", "yh")


def moves(target):
    pairs = []
    for number in range(math.prod(SIZES)):
        rest, spot = number, []
        for size in reversed(SIZES):
            spot.append(rest % size)
            rest //= size
        goal = 0
        for size, value in zip(SIZES, target(*reversed(spot))):
            goal = goal * size + value
        pairs.append((number, goal))
    return pairs


def weight_target(z, yl, c, x, yh):
    return (z, 1 - yl, yh, x, c)


def core_target(z, yl, c, x, yh):
    return (z, yl, 1 - c, x, yh)


def along_y(distance):
    def target(z, yl, c, x, yh):
        y = (yl + 2 * yh + distance) % Y_SIZE
        return (z, y % 2, c, x, y // 2)

    return target


def params(mib):
    return pltpu.CompilerParams(vmem_limit_bytes=mib << 20)


def pack_kernel(q_ref, k_ref, v_ref, seg_ref, out_ref):
    seg = jnp.broadcast_to(seg_ref[...].astype(f32), (SEG_ROWS, ROWS)).astype(bf16)
    for head in range(HEADS):
        lanes = slice(head * HEAD_DIM, (head + 1) * HEAD_DIM)
        out_ref[head, 0:ROWS, :] = q_ref[:, lanes]
        out_ref[head, ROWS : 2 * ROWS, :] = k_ref[:, lanes]
        out_ref[head, 2 * ROWS : 3 * ROWS, :] = v_ref[:, lanes]
        out_ref[head, 3 * ROWS :, :] = seg


def attend_kernel(x_ref, out_ref):
    blocks = x_ref.shape[0]
    seg = x_ref[:, 3 * ROWS :, :].astype(f32)
    first = (jnp.sum(jnp.where(seg < 0.5, 1.0, 0.0)) * (1.0 / SEG_ROWS)).astype(jnp.int32)
    second = (jnp.sum(jnp.where(seg < 1.5, 1.0, 0.0)) * (1.0 / SEG_ROWS)).astype(jnp.int32)
    per = Q_BLOCK // ROWS
    for block in range(blocks // per):
        start = block * per
        low = max(0, start - SEG_MOST // ROWS)
        high = start + per
        width = (high - low) * ROWS
        query = x_ref[start:high, 0:ROWS, :].reshape(Q_BLOCK, HEAD_DIM)
        key = x_ref[low:high, ROWS : 2 * ROWS, :].reshape(width, HEAD_DIM)
        value = x_ref[low:high, 2 * ROWS : 3 * ROWS, :].reshape(width, HEAD_DIM)
        scores = lax.dot_general(
            query, key, (((1,), (1,)), ((), ())), preferred_element_type=f32
        ) * HEAD_DIM ** (-0.5)
        row = start * ROWS + lax.broadcasted_iota(jnp.int32, (Q_BLOCK, 1), 0)
        column = low * ROWS + lax.broadcasted_iota(jnp.int32, (Q_BLOCK, width), 1)
        begin = jnp.where(row < first, 0, jnp.where(row < second, first, second))
        allowed = (column <= row) & (column >= begin)
        scores = jnp.where(allowed, scores, NEG_FILL)
        top = jnp.max(scores, axis=-1, keepdims=True)
        probs = jnp.exp(scores - top)
        total = jnp.sum(probs, axis=-1, keepdims=True)
        mixed = jnp.dot(probs.astype(bf16), value, preferred_element_type=f32)
        out_ref[start:high] = (mixed / total).astype(bf16).reshape(per, ROWS, HEAD_DIM)


def place_of(expert):
    return (expert & 48) | (8 - (expert & 8)) | ((expert & 3) << 1) | ((expert >> 2) & 1)


def reach_of(expert, y):
    distance = (1 - ((expert >> 3) & 1) + ((expert >> 1) & 2) - y) & 3
    return (distance << 4) | ((expert >> 2) & 12) | (expert & 3)


def route_kernel(y_ref, ids_ref, codes_ref, pick_ref, weight_ref):
    number = lax.broadcasted_iota(jnp.int32, (EXPERTS, ROWS), 0)
    earlier = lax.broadcasted_iota(jnp.int32, (ROWS, ROWS), 0) < lax.broadcasted_iota(
        jnp.int32, (ROWS, ROWS), 1
    )
    earlier = jnp.where(earlier, 1.0, 0.0).astype(bf16)
    rows = EXPERTS * SLOTS
    own = lax.broadcasted_iota(jnp.int32, (rows, EXPERTS), 0) // SLOTS
    mine = own == lax.broadcasted_iota(jnp.int32, (rows, EXPERTS), 1)
    mine = jnp.where(mine, 1.0, 0.0).astype(bf16)
    slot = (lax.broadcasted_iota(jnp.int32, (rows, ROWS), 0) & (SLOTS - 1)) + 1
    ids = ids_ref[...]

    def ordered(names):
        member = jnp.zeros((EXPERTS, ROWS), f32)
        code = jnp.zeros((EXPERTS, ROWS), f32)
        for k in range(TOPK):
            named = number == names[k : k + 1, :]
            member = member + jnp.where(named, 1.0, 0.0)
            code = code + jnp.where(named, codes_ref[k : k + 1, :].astype(f32), 0.0)
        rank = jnp.dot(member.astype(bf16), earlier, preferred_element_type=f32)
        place = jnp.dot(mine, (member * (rank + 1.0)).astype(bf16), preferred_element_type=f32)
        return place == slot.astype(f32), code

    here, _ = ordered(reach_of(ids, y_ref[0]))
    pick_ref[...] = jnp.where(here, 1.0, 0.0).astype(bf16)
    here, code = ordered(place_of(ids))
    codes = jnp.dot(mine, code.astype(bf16), preferred_element_type=f32)
    weight_ref[...] = jnp.where(here, codes, 0.0).astype(bf16)


K_STEPS = 4


def project_kernel(heads_ref, weight_ref, hidden_ref, gain_ref, pick_ref, mixed_ref, *rest):
    shares, own_ref, acc = rest[:3], rest[3], rest[4]
    step = pl.program_id(0)
    per = HEADS // K_STEPS
    part = jnp.concatenate([heads_ref[i] for i in range(per)], axis=1)
    product = jnp.dot(part, weight_ref[...], preferred_element_type=f32)

    @pl.when(step == 0)
    def _():
        acc[...] = product
        for distance in range(1, Y_SIZE):
            for spot in range(SPOTS):
                lanes = slice(spot * ROWS, (spot + 1) * ROWS)
                first = (distance * SPOTS + spot) * SLOTS
                shares[distance - 1][ROWS:, lanes] = pick_ref[first : first + SLOTS, :]

    @pl.when(step > 0)
    def _():
        acc[...] += product

    @pl.when(step == K_STEPS - 1)
    def _():
        mixed = (hidden_ref[...].astype(f32) + acc[...]).astype(bf16)
        mixed_ref[...] = mixed
        wide = mixed.astype(f32)
        scale = lax.rsqrt(jnp.mean(wide * wide, axis=-1, keepdims=True) + 1e-06)
        normed = (wide * scale * gain_ref[...]).astype(bf16)
        for share_ref in shares:
            share_ref[0:ROWS, :] = normed
        picked = jnp.dot(pick_ref[: SPOTS * SLOTS, :], normed, preferred_element_type=f32)
        own_ref[...] = picked.astype(bf16).reshape(SPOTS, SLOTS, D)


def fill_kernel(near_ref, far_ref, back_ref, send_ref, rows, sems):
    copies = []
    for source, share_ref in enumerate((near_ref, back_ref, far_ref)):
        picks = [share_ref[ROWS:, i * ROWS : (i + 1) * ROWS] for i in range(SPOTS)]
        picked = jnp.dot(
            jnp.concatenate(picks, axis=0), share_ref[0:ROWS, :], preferred_element_type=f32
        )
        rows[source] = picked.astype(bf16).reshape(SPOTS, SLOTS, D)
        copy = pltpu.make_async_copy(rows.at[source], send_ref.at[:, source], sems.at[source])
        copy.start()
        copies.append(copy)
    for copy in copies:
        copy.wait()


def origin(unit):
    if unit < SPOTS:
        return unit, 0
    return (unit - SPOTS) // 3, (3, 1, 2)[(unit - SPOTS) % 3]


def inner_kernel(rows_ref, *refs):
    pieces = len(PIECES)
    parts, (act, w_in, sems) = refs[:pieces], refs[pieces:]
    copies, start = [], 0
    for number, (part, count) in enumerate(zip(parts, PIECES)):
        goal = w_in.at[pl.ds(start, count)]
        copies.append(pltpu.make_async_copy(part, goal, sems.at[number]))
        start += count
    for copy in copies:
        copy.start()
    for copy in copies:
        copy.wait()
    for block in range(rows_ref.shape[0] // X_BLOCK):
        span = slice(block * X_BLOCK, (block + 1) * X_BLOCK)
        inner = jnp.dot(rows_ref[span, :], w_in[...], preferred_element_type=f32)
        gate = inner[:, :HALF]
        up = pltpu.roll(inner, HALF, axis=1)[:, :HALF]
        act[span, :] = (gate / (1.0 + jnp.exp(-gate)) * up).astype(bf16)


def down_kernel(y_ref, own_a, own_b, rest_a, rest_b, down_a, down_b, out_ref):
    y = y_ref[0]
    units = X_BLOCK // SLOTS
    for block in range(EXPERTS * SLOTS // X_BLOCK):
        act_a, act_b, first = (own_a, own_b, 0) if block == 0 else (rest_a, rest_b, block - 1)
        span = slice(first * X_BLOCK, (first + 1) * X_BLOCK)
        total = jnp.dot(act_a[span, :], down_a[...], preferred_element_type=f32)
        total = total + jnp.dot(act_b[span, :], down_b[...], preferred_element_type=f32)
        total = total.astype(bf16)
        for near in range(units):
            spot, ahead = origin(block * units + near)
            from_y = (y + ahead) & 3
            rows = total[near * SLOTS : (near + 1) * SLOTS, :]
            out_ref[spot // 4, from_y & 1, spot % 4, from_y >> 1] = rows


def combine_kernel(rows_ref, weight_ref, mixed_ref, out_ref, acc, total):
    step = pl.program_id(0)
    over = (((0,), (0,)), ((), ()))
    weight = weight_ref[...]
    product = lax.dot_general(weight, rows_ref[...], over, preferred_element_type=f32)
    ones = jnp.ones((weight.shape[0], ROWS), bf16)
    count = lax.dot_general(weight, ones, over, preferred_element_type=f32)

    @pl.when(step == 0)
    def _():
        acc[...] = product
        total[...] = count

    @pl.when(step > 0)
    def _():
        acc[...] += product
        total[...] += count

    @pl.when(step == pl.num_programs(0) - 1)
    def _():
        routed = acc[...] / total[:, 0:1]
        out_ref[...] = (mixed_ref[...].astype(f32) + routed).astype(bf16)


def local(
    queries,
    keys,
    values,
    segment_ids,
    hidden_in,
    out_weight,
    norm_gain,
    expert_ids,
    gate_codes,
    w_in,
    w_down,
):
    shape = jax.ShapeDtypeStruct
    y = (lax.axis_index("yl") + 2 * lax.axis_index("yh")).astype(jnp.int32)[None]
    gate_up, start, moved, other = w_in[0], 0, [], []
    for count in PIECES:
        piece = lax.slice_in_dim(gate_up, start, start + count)
        moved.append(lax.ppermute(piece, AXES, moves(weight_target)))
        other.append(lax.ppermute(moved[-1], AXES, moves(core_target)))
        start += count
    moved_down = lax.ppermute(w_down[0], AXES, moves(weight_target))
    other_down = lax.ppermute(moved_down, AXES, moves(core_target))
    packed = pl.pallas_call(
        pack_kernel,
        out_shape=shape((HEADS, PACK_ROWS, HEAD_DIM), bf16),
        in_specs=[VMEM] * 4,
        out_specs=VMEM,
        compiler_params=params(60),
        name="pack",
    )(queries[0], keys[0], values[0], segment_ids)
    swapped = lax.all_to_all(packed, POSITIONS, split_axis=0, concat_axis=0, tiled=True)
    attended = pl.pallas_call(
        attend_kernel,
        out_shape=shape((HEADS, ROWS, HEAD_DIM), bf16),
        in_specs=[VMEM],
        out_specs=VMEM,
        compiler_params=params(40),
        name="attend",
    )(swapped)
    heads = lax.all_to_all(attended, POSITIONS, split_axis=0, concat_axis=0, tiled=True)
    pick, weight = pl.pallas_call(
        route_kernel,
        out_shape=(
            shape((EXPERTS * SLOTS, ROWS), bf16),
            shape((EXPERTS * SLOTS, ROWS), bf16),
        ),
        in_specs=[SMEM, VMEM, VMEM],
        out_specs=(VMEM, VMEM),
        compiler_params=params(60),
        name="route",
    )(y, expert_ids[0].T, gate_codes[0].T)
    per = HEADS // K_STEPS
    share_shape = (ROWS + SLOTS, D)
    mixed, *shares, own = pl.pallas_call(
        project_kernel,
        grid=(K_STEPS,),
        out_shape=(
            shape((ROWS, D), bf16),
            shape(share_shape, bf16),
            shape(share_shape, bf16),
            shape(share_shape, bf16),
            shape((SPOTS, SLOTS, D), bf16),
        ),
        in_specs=[
            pl.BlockSpec((per, ROWS, HEAD_DIM), lambda i: (i, 0, 0)),
            pl.BlockSpec((D // K_STEPS, D), lambda i: (i, 0)),
            pl.BlockSpec((ROWS, D), lambda i: (0, 0)),
            pl.BlockSpec((1, D), lambda i: (0, 0)),
            pl.BlockSpec((EXPERTS * SLOTS, ROWS), lambda i: (0, 0)),
        ],
        out_specs=(
            pl.BlockSpec((ROWS, D), lambda i: (0, 0)),
            pl.BlockSpec(share_shape, lambda i: (0, 0)),
            pl.BlockSpec(share_shape, lambda i: (0, 0)),
            pl.BlockSpec(share_shape, lambda i: (0, 0)),
            pl.BlockSpec((SPOTS, SLOTS, D), lambda i: (0, 0, 0)),
        ),
        scratch_shapes=[pltpu.VMEM((ROWS, D), f32)],
        compiler_params=params(53),
        name="project",
    )(heads, out_weight, hidden_in[0], norm_gain[None], pick)
    arriving = []
    for distance, share in enumerate(shares, 1):
        arriving.append(lax.ppermute(share, AXES, moves(along_y(distance))))
    arrived_own = lax.all_to_all(own, ("z", "x"), split_axis=0, concat_axis=0, tiled=True)
    near, far, back = arriving
    send = pl.pallas_call(
        fill_kernel,
        out_shape=shape((SPOTS, 3, SLOTS, D), bf16),
        in_specs=[VMEM] * 3,
        out_specs=pl.BlockSpec(memory_space=pl.ANY),
        scratch_shapes=[
            pltpu.VMEM((3, SPOTS, SLOTS, D), bf16),
            pltpu.SemaphoreType.DMA((3,)),
        ],
        compiler_params=params(50),
        name="fill",
    )(near, far, back)
    arrived = lax.all_to_all(
        send.reshape(SPOTS, 3 * SLOTS, D), ("z", "x"), split_axis=0, concat_axis=0, tiled=True
    )
    anywhere = pl.BlockSpec(memory_space=pl.ANY)

    def inner(rows, parts):
        rows = rows.reshape(-1, D)
        return pl.pallas_call(
            inner_kernel,
            out_shape=shape((rows.shape[0], HALF), bf16),
            in_specs=[VMEM] + [anywhere] * len(PIECES),
            out_specs=VMEM,
            scratch_shapes=[
                pltpu.VMEM((D, 2 * HALF), bf16),
                pltpu.SemaphoreType.DMA((len(PIECES),)),
            ],
            compiler_params=params(32),
        )(rows, *parts)

    own_a = inner(arrived_own, moved)
    own_b = inner(arrived_own, other)
    rest_a = inner(arrived, moved)
    rest_b = inner(arrived, other)
    results = pl.pallas_call(
        down_kernel,
        out_shape=shape((4, 2, 4, 2, SLOTS, D), bf16),
        in_specs=[SMEM] + [VMEM] * 6,
        out_specs=VMEM,
        compiler_params=params(32),
        name="down",
    )(y, own_a, own_b, rest_a, rest_b, moved_down, other_down)
    returned = lax.all_to_all(
        results.reshape(EXPERTS, SLOTS, D), PLACES, split_axis=0, concat_axis=0, tiled=True
    )
    block = 256
    layer_out = pl.pallas_call(
        combine_kernel,
        grid=(EXPERTS * SLOTS // block,),
        out_shape=shape((ROWS, D), bf16),
        in_specs=[
            pl.BlockSpec((block, D), lambda i: (i, 0)),
            pl.BlockSpec((block, ROWS), lambda i: (i, 0)),
            pl.BlockSpec((ROWS, D), lambda i: (0, 0)),
        ],
        out_specs=pl.BlockSpec((ROWS, D), lambda i: (0, 0)),
        scratch_shapes=[pltpu.VMEM((ROWS, D), f32), pltpu.VMEM((ROWS, ROWS), f32)],
        compiler_params=params(12),
        name="combine",
    )(returned.reshape(EXPERTS * SLOTS, D), weight, mixed)
    return layer_out[None]


def solution(mesh):
    parts = Mesh(mesh.devices.reshape(SIZES), AXES)
    rows = P(STREAM, POSITIONS, None)
    owned = P((*POSITIONS, *STREAM), None, None)
    placed = (rows, rows, rows, P(STREAM, POSITIONS), rows, P(), P(), rows, rows, owned, owned)
    return jax.shard_map(local, mesh=parts, in_specs=placed, out_specs=rows, check_vma=False)
```

```python
import math

import jax
import jax.numpy as jnp
from jax import lax
from jax.experimental import pallas as pl
from jax.experimental.pallas import tpu as pltpu
from jax.sharding import Mesh
from jax.sharding import PartitionSpec as P

D = 2048
HEADS = 16
HEAD_DIM = 128
TOPK = 6
ROWS = 128
EXPERTS = 64
SLOTS = 16
HALF = 704
SEG_MOST = 1024
SEG_ROWS = 16
PACK_ROWS = 3 * ROWS + SEG_ROWS
Q_BLOCK = 256
X_BLOCK = 256
PACK_STEPS = 4
PIECES = (256, 384, 448, 960)
SPOTS = 16
Y_SIZE = 4
NEG_FILL = -1e30

VMEM = pl.BlockSpec(memory_space=pltpu.VMEM)
SMEM = pl.BlockSpec(memory_space=pltpu.SMEM)
f32 = jnp.float32
bf16 = jnp.bfloat16


SIZES = (4, 2, 2, 4, 2)
AXES = ("z", "yl", "c", "x", "yh")
POSITIONS = ("z", "yl", "c")
STREAM = ("x", "yh")
PLACES = ("z", "yl", "x", "yh")


def moves(target):
    pairs = []
    for number in range(math.prod(SIZES)):
        rest, spot = number, []
        for size in reversed(SIZES):
            spot.append(rest % size)
            rest //= size
        goal = 0
        for size, value in zip(SIZES, target(*reversed(spot))):
            goal = goal * size + value
        pairs.append((number, goal))
    return pairs


def weight_target(z, yl, c, x, yh):
    return (z, 1 - yl, yh, x, c)


def core_target(z, yl, c, x, yh):
    return (z, yl, 1 - c, x, yh)


def along_y(distance):
    def target(z, yl, c, x, yh):
        y = (yl + 2 * yh + distance) % Y_SIZE
        return (z, y % 2, c, x, y // 2)

    return target


def params(mib):
    return pltpu.CompilerParams(vmem_limit_bytes=mib << 20)


def pack_kernel(q_ref, k_ref, v_ref, seg_ref, out_ref):
    seg = jnp.broadcast_to(seg_ref[...].astype(f32), (SEG_ROWS, ROWS)).astype(bf16)
    for head in range(HEADS // PACK_STEPS):
        lanes = slice(head * HEAD_DIM, (head + 1) * HEAD_DIM)
        out_ref[head, 0:ROWS, :] = q_ref[:, lanes]
        out_ref[head, ROWS : 2 * ROWS, :] = k_ref[:, lanes]
        out_ref[head, 2 * ROWS : 3 * ROWS, :] = v_ref[:, lanes]
        out_ref[head, 3 * ROWS :, :] = seg


def attend_kernel(x_ref, out_ref):
    blocks = x_ref.shape[0]
    seg = x_ref[:, 3 * ROWS :, :].astype(f32)
    first = (jnp.sum(jnp.where(seg < 0.5, 1.0, 0.0)) * (1.0 / SEG_ROWS)).astype(jnp.int32)
    second = (jnp.sum(jnp.where(seg < 1.5, 1.0, 0.0)) * (1.0 / SEG_ROWS)).astype(jnp.int32)
    per = Q_BLOCK // ROWS
    for block in range(blocks // per):
        start = block * per
        low = max(0, start - SEG_MOST // ROWS)
        high = start + per
        width = (high - low) * ROWS
        query = x_ref[start:high, 0:ROWS, :].reshape(Q_BLOCK, HEAD_DIM)
        key = x_ref[low:high, ROWS : 2 * ROWS, :].reshape(width, HEAD_DIM)
        value = x_ref[low:high, 2 * ROWS : 3 * ROWS, :].reshape(width, HEAD_DIM)
        scores = lax.dot_general(
            query, key, (((1,), (1,)), ((), ())), preferred_element_type=f32
        ) * HEAD_DIM ** (-0.5)
        row = start * ROWS + lax.broadcasted_iota(jnp.int32, (Q_BLOCK, 1), 0)
        column = low * ROWS + lax.broadcasted_iota(jnp.int32, (Q_BLOCK, width), 1)
        begin = jnp.where(row < first, 0, jnp.where(row < second, first, second))
        allowed = (column <= row) & (column >= begin)
        scores = jnp.where(allowed, scores, NEG_FILL)
        top = jnp.max(scores, axis=-1, keepdims=True)
        probs = jnp.exp(scores - top)
        total = jnp.sum(probs, axis=-1, keepdims=True)
        mixed = jnp.dot(probs.astype(bf16), value, preferred_element_type=f32)
        out_ref[start:high] = (mixed / total).astype(bf16).reshape(per, ROWS, HEAD_DIM)


def place_of(expert):
    return (expert & 48) | (8 - (expert & 8)) | ((expert & 3) << 1) | ((expert >> 2) & 1)


def reach_of(expert, y):
    distance = (1 - ((expert >> 3) & 1) + ((expert >> 1) & 2) - y) & 3
    return (distance << 4) | ((expert >> 2) & 12) | (expert & 3)


def route_kernel(y_ref, ids_ref, codes_ref, pick_ref, weight_ref):
    number = lax.broadcasted_iota(jnp.int32, (EXPERTS, ROWS), 0)
    earlier = lax.broadcasted_iota(jnp.int32, (ROWS, ROWS), 0) < lax.broadcasted_iota(
        jnp.int32, (ROWS, ROWS), 1
    )
    earlier = jnp.where(earlier, 1.0, 0.0).astype(bf16)
    rows = EXPERTS * SLOTS
    own = lax.broadcasted_iota(jnp.int32, (rows, EXPERTS), 0) // SLOTS
    mine = own == lax.broadcasted_iota(jnp.int32, (rows, EXPERTS), 1)
    mine = jnp.where(mine, 1.0, 0.0).astype(bf16)
    slot = (lax.broadcasted_iota(jnp.int32, (rows, ROWS), 0) & (SLOTS - 1)) + 1
    ids = ids_ref[...]

    def ordered(names):
        member = jnp.zeros((EXPERTS, ROWS), f32)
        code = jnp.zeros((EXPERTS, ROWS), f32)
        for k in range(TOPK):
            named = number == names[k : k + 1, :]
            member = member + jnp.where(named, 1.0, 0.0)
            code = code + jnp.where(named, codes_ref[k : k + 1, :].astype(f32), 0.0)
        rank = jnp.dot(member.astype(bf16), earlier, preferred_element_type=f32)
        place = jnp.dot(mine, (member * (rank + 1.0)).astype(bf16), preferred_element_type=f32)
        return place == slot.astype(f32), code

    here, _ = ordered(reach_of(ids, y_ref[0]))
    pick_ref[...] = jnp.where(here, 1.0, 0.0).astype(bf16)
    here, code = ordered(place_of(ids))
    codes = jnp.dot(mine, code.astype(bf16), preferred_element_type=f32)
    weight_ref[...] = jnp.where(here, codes, 0.0).astype(bf16)


K_STEPS = 4


def project_kernel(heads_ref, weight_ref, hidden_ref, gain_ref, pick_ref, mixed_ref, *rest):
    shares, own_ref, acc = rest[:3], rest[3], rest[4]
    step = pl.program_id(0)
    per = HEADS // K_STEPS
    part = jnp.concatenate([heads_ref[i] for i in range(per)], axis=1)
    product = jnp.dot(part, weight_ref[...], preferred_element_type=f32)

    @pl.when(step == 0)
    def _():
        acc[...] = product
        for distance in range(1, Y_SIZE):
            for spot in range(SPOTS):
                lanes = slice(spot * ROWS, (spot + 1) * ROWS)
                first = (distance * SPOTS + spot) * SLOTS
                shares[distance - 1][ROWS:, lanes] = pick_ref[first : first + SLOTS, :]

    @pl.when(step > 0)
    def _():
        acc[...] += product

    @pl.when(step == K_STEPS - 1)
    def _():
        mixed = (hidden_ref[...].astype(f32) + acc[...]).astype(bf16)
        mixed_ref[...] = mixed
        wide = mixed.astype(f32)
        scale = lax.rsqrt(jnp.mean(wide * wide, axis=-1, keepdims=True) + 1e-06)
        normed = (wide * scale * gain_ref[...]).astype(bf16)
        for share_ref in shares:
            share_ref[0:ROWS, :] = normed
        picked = jnp.dot(pick_ref[: SPOTS * SLOTS, :], normed, preferred_element_type=f32)
        own_ref[...] = picked.astype(bf16).reshape(SPOTS, SLOTS, D)


def fill_kernel(near_ref, far_ref, back_ref, send_ref, rows, sems):
    copies = []
    for source, share_ref in enumerate((near_ref, back_ref, far_ref)):
        picks = [share_ref[ROWS:, i * ROWS : (i + 1) * ROWS] for i in range(SPOTS)]
        picked = jnp.dot(
            jnp.concatenate(picks, axis=0), share_ref[0:ROWS, :], preferred_element_type=f32
        )
        rows[source] = picked.astype(bf16).reshape(SPOTS, SLOTS, D)
        copy = pltpu.make_async_copy(rows.at[source], send_ref.at[:, source], sems.at[source])
        copy.start()
        copies.append(copy)
    for copy in copies:
        copy.wait()


def origin(unit):
    if unit < SPOTS:
        return unit, 0
    return (unit - SPOTS) // 3, (3, 1, 2)[(unit - SPOTS) % 3]


def inner_kernel(rows_ref, *refs):
    pieces = len(PIECES)
    parts, (act, w_in, sems) = refs[:pieces], refs[pieces:]
    copies, start = [], 0
    for number, (part, count) in enumerate(zip(parts, PIECES)):
        goal = w_in.at[pl.ds(start, count)]
        copies.append(pltpu.make_async_copy(part, goal, sems.at[number]))
        start += count
    for copy in copies:
        copy.start()
    for copy in copies:
        copy.wait()
    for block in range(rows_ref.shape[0] // X_BLOCK):
        span = slice(block * X_BLOCK, (block + 1) * X_BLOCK)
        inner = jnp.dot(rows_ref[span, :], w_in[...], preferred_element_type=f32)
        gate = inner[:, :HALF]
        up = pltpu.roll(inner, HALF, axis=1)[:, :HALF]
        act[span, :] = (gate / (1.0 + jnp.exp(-gate)) * up).astype(bf16)


def down_kernel(y_ref, own_a, own_b, rest_a, rest_b, down_a, down_b, out_ref):
    y = y_ref[0]
    units = X_BLOCK // SLOTS
    for block in range(EXPERTS * SLOTS // X_BLOCK):
        act_a, act_b, first = (own_a, own_b, 0) if block == 0 else (rest_a, rest_b, block - 1)
        span = slice(first * X_BLOCK, (first + 1) * X_BLOCK)
        total = jnp.dot(act_a[span, :], down_a[...], preferred_element_type=f32)
        total = total + jnp.dot(act_b[span, :], down_b[...], preferred_element_type=f32)
        total = total.astype(bf16)
        for near in range(units):
            spot, ahead = origin(block * units + near)
            from_y = (y + ahead) & 3
            rows = total[near * SLOTS : (near + 1) * SLOTS, :]
            out_ref[spot // 4, from_y & 1, spot % 4, from_y >> 1] = rows


def combine_kernel(rows_ref, weight_ref, mixed_ref, out_ref):
    over = (((0,), (0,)), ((), ()))
    weight = weight_ref[...]
    routed = lax.dot_general(weight, rows_ref[...], over, preferred_element_type=f32)
    ones = jnp.ones((weight.shape[0], ROWS), bf16)
    total = lax.dot_general(weight, ones, over, preferred_element_type=f32)
    out_ref[...] = (mixed_ref[...].astype(f32) + routed / total[:, 0:1]).astype(bf16)


def local(
    queries,
    keys,
    values,
    segment_ids,
    hidden_in,
    out_weight,
    norm_gain,
    expert_ids,
    gate_codes,
    w_in,
    w_down,
):
    shape = jax.ShapeDtypeStruct
    y = (lax.axis_index("yl") + 2 * lax.axis_index("yh")).astype(jnp.int32)[None]
    gate_up, start, moved, other = w_in[0], 0, [], []
    for count in PIECES:
        piece = lax.slice_in_dim(gate_up, start, start + count)
        moved.append(lax.ppermute(piece, AXES, moves(weight_target)))
        other.append(lax.ppermute(moved[-1], AXES, moves(core_target)))
        start += count
    moved_down = lax.ppermute(w_down[0], AXES, moves(weight_target))
    other_down = lax.ppermute(moved_down, AXES, moves(core_target))
    wide = pl.BlockSpec((ROWS, D // PACK_STEPS), lambda i: (0, i))
    packed = pl.pallas_call(
        pack_kernel,
        grid=(PACK_STEPS,),
        out_shape=shape((HEADS, PACK_ROWS, HEAD_DIM), bf16),
        in_specs=[wide, wide, wide, pl.BlockSpec((1, ROWS), lambda i: (0, 0))],
        out_specs=pl.BlockSpec((HEADS // PACK_STEPS, PACK_ROWS, HEAD_DIM), lambda i: (i, 0, 0)),
        compiler_params=params(60),
        name="pack",
    )(queries[0], keys[0], values[0], segment_ids)
    swapped = lax.all_to_all(packed, POSITIONS, split_axis=0, concat_axis=0, tiled=True)
    attended = pl.pallas_call(
        attend_kernel,
        out_shape=shape((HEADS, ROWS, HEAD_DIM), bf16),
        in_specs=[VMEM],
        out_specs=VMEM,
        compiler_params=params(40),
        name="attend",
    )(swapped)
    heads = lax.all_to_all(attended, POSITIONS, split_axis=0, concat_axis=0, tiled=True)
    pick, weight = pl.pallas_call(
        route_kernel,
        out_shape=(
            shape((EXPERTS * SLOTS, ROWS), bf16),
            shape((EXPERTS * SLOTS, ROWS), bf16),
        ),
        in_specs=[SMEM, VMEM, VMEM],
        out_specs=(VMEM, VMEM),
        compiler_params=params(60),
        name="route",
    )(y, expert_ids[0].T, gate_codes[0].T)
    per = HEADS // K_STEPS
    share_shape = (ROWS + SLOTS, D)
    mixed, *shares, own = pl.pallas_call(
        project_kernel,
        grid=(K_STEPS,),
        out_shape=(
            shape((ROWS, D), bf16),
            shape(share_shape, bf16),
            shape(share_shape, bf16),
            shape(share_shape, bf16),
            shape((SPOTS, SLOTS, D), bf16),
        ),
        in_specs=[
            pl.BlockSpec((per, ROWS, HEAD_DIM), lambda i: (i, 0, 0)),
            pl.BlockSpec((D // K_STEPS, D), lambda i: (i, 0)),
            pl.BlockSpec((ROWS, D), lambda i: (0, 0)),
            pl.BlockSpec((1, D), lambda i: (0, 0)),
            pl.BlockSpec((EXPERTS * SLOTS, ROWS), lambda i: (0, 0)),
        ],
        out_specs=(
            pl.BlockSpec((ROWS, D), lambda i: (0, 0)),
            pl.BlockSpec(share_shape, lambda i: (0, 0)),
            pl.BlockSpec(share_shape, lambda i: (0, 0)),
            pl.BlockSpec(share_shape, lambda i: (0, 0)),
            pl.BlockSpec((SPOTS, SLOTS, D), lambda i: (0, 0, 0)),
        ),
        scratch_shapes=[pltpu.VMEM((ROWS, D), f32)],
        compiler_params=params(50),
        name="project",
    )(heads, out_weight, hidden_in[0], norm_gain[None], pick)
    arriving = []
    for distance, share in enumerate(shares, 1):
        arriving.append(lax.ppermute(share, AXES, moves(along_y(distance))))
    arrived_own = lax.all_to_all(own, ("z", "x"), split_axis=0, concat_axis=0, tiled=True)
    near, far, back = arriving
    send = pl.pallas_call(
        fill_kernel,
        out_shape=shape((SPOTS, 3, SLOTS, D), bf16),
        in_specs=[VMEM] * 3,
        out_specs=pl.BlockSpec(memory_space=pl.ANY),
        scratch_shapes=[
            pltpu.VMEM((3, SPOTS, SLOTS, D), bf16),
            pltpu.SemaphoreType.DMA((3,)),
        ],
        compiler_params=params(50),
        name="fill",
    )(near, far, back)
    arrived = lax.all_to_all(
        send.reshape(SPOTS, 3 * SLOTS, D), ("z", "x"), split_axis=0, concat_axis=0, tiled=True
    )
    anywhere = pl.BlockSpec(memory_space=pl.ANY)

    def inner(rows, parts):
        rows = rows.reshape(-1, D)
        return pl.pallas_call(
            inner_kernel,
            out_shape=shape((rows.shape[0], HALF), bf16),
            in_specs=[VMEM] + [anywhere] * len(PIECES),
            out_specs=VMEM,
            scratch_shapes=[
                pltpu.VMEM((D, 2 * HALF), bf16),
                pltpu.SemaphoreType.DMA((len(PIECES),)),
            ],
            compiler_params=params(32),
        )(rows, *parts)

    own_a = inner(arrived_own, moved)
    own_b = inner(arrived_own, other)
    rest_a = inner(arrived, moved)
    rest_b = inner(arrived, other)
    results = pl.pallas_call(
        down_kernel,
        out_shape=shape((4, 2, 4, 2, SLOTS, D), bf16),
        in_specs=[SMEM] + [VMEM] * 6,
        out_specs=VMEM,
        compiler_params=params(32),
        name="down",
    )(y, own_a, own_b, rest_a, rest_b, moved_down, other_down)
    returned = lax.all_to_all(
        results.reshape(EXPERTS, SLOTS, D), PLACES, split_axis=0, concat_axis=0, tiled=True
    )
    layer_out = pl.pallas_call(
        combine_kernel,
        out_shape=shape((ROWS, D), bf16),
        in_specs=[VMEM] * 3,
        out_specs=VMEM,
        compiler_params=params(24),
        name="combine",
    )(returned.reshape(EXPERTS * SLOTS, D), weight, mixed)
    return layer_out[None]


def solution(mesh):
    parts = Mesh(mesh.devices.reshape(SIZES), AXES)
    rows = P(STREAM, POSITIONS, None)
    owned = P((*POSITIONS, *STREAM), None, None)
    placed = (rows, rows, rows, P(STREAM, POSITIONS), rows, P(), P(), rows, rows, owned, owned)
    return jax.shard_map(local, mesh=parts, in_specs=placed, out_specs=rows, check_vma=False)
```

```python
import functools
import math

import jax
import jax.numpy as jnp
from jax import lax
from jax.experimental import pallas as pl
from jax.experimental.pallas import tpu as pltpu
from jax.sharding import Mesh
from jax.sharding import PartitionSpec as P

D = 2048
HEADS = 16
HEAD_DIM = 128
TOPK = 6
ROWS = 128
EXPERTS = 64
SLOTS = 16
HALF = 704
SEG_MOST = 1024
SEG_ROWS = 16
PACK_ROWS = 3 * ROWS + SEG_ROWS
Q_BLOCK = 256
X_BLOCK = 256
PIECES = (256, 384, 448, 960)
SPOTS = 16
Y_SIZE = 4
NEG_FILL = -1e30

VMEM = pl.BlockSpec(memory_space=pltpu.VMEM)
SMEM = pl.BlockSpec(memory_space=pltpu.SMEM)
f32 = jnp.float32
bf16 = jnp.bfloat16


SIZES = (4, 2, 2, 4, 2)
AXES = ("z", "yl", "c", "x", "yh")
POSITIONS = ("z", "yl", "c")
STREAM = ("x", "yh")
PLACES = ("z", "yl", "x", "yh")


def moves(target):
    pairs = []
    for number in range(math.prod(SIZES)):
        rest, spot = number, []
        for size in reversed(SIZES):
            spot.append(rest % size)
            rest //= size
        goal = 0
        for size, value in zip(SIZES, target(*reversed(spot))):
            goal = goal * size + value
        pairs.append((number, goal))
    return pairs


def weight_target(z, yl, c, x, yh):
    return (z, 1 - yl, yh, x, c)


def core_target(z, yl, c, x, yh):
    return (z, yl, 1 - c, x, yh)


def along_y(distance):
    def target(z, yl, c, x, yh):
        y = (yl + 2 * yh + distance) % Y_SIZE
        return (z, y % 2, c, x, y // 2)

    return target


def params(mib):
    return pltpu.CompilerParams(vmem_limit_bytes=mib << 20)


def pack_kernel(q_ref, k_ref, v_ref, seg_ref, out_ref):
    seg = jnp.broadcast_to(seg_ref[...].astype(f32), (SEG_ROWS, ROWS)).astype(bf16)
    for head in range(HEADS):
        lanes = slice(head * HEAD_DIM, (head + 1) * HEAD_DIM)
        out_ref[head, 0:ROWS, :] = q_ref[:, lanes]
        out_ref[head, ROWS : 2 * ROWS, :] = k_ref[:, lanes]
        out_ref[head, 2 * ROWS : 3 * ROWS, :] = v_ref[:, lanes]
        out_ref[head, 3 * ROWS :, :] = seg


def attend_kernel(x_ref, out_ref):
    blocks = x_ref.shape[0]
    seg = x_ref[:, 3 * ROWS :, :].astype(f32)
    first = (jnp.sum(jnp.where(seg < 0.5, 1.0, 0.0)) * (1.0 / SEG_ROWS)).astype(jnp.int32)
    second = (jnp.sum(jnp.where(seg < 1.5, 1.0, 0.0)) * (1.0 / SEG_ROWS)).astype(jnp.int32)
    per = Q_BLOCK // ROWS
    for block in range(blocks // per):
        start = block * per
        low = max(0, start - SEG_MOST // ROWS)
        high = start + per
        width = (high - low) * ROWS
        query = x_ref[start:high, 0:ROWS, :].reshape(Q_BLOCK, HEAD_DIM)
        key = x_ref[low:high, ROWS : 2 * ROWS, :].reshape(width, HEAD_DIM)
        value = x_ref[low:high, 2 * ROWS : 3 * ROWS, :].reshape(width, HEAD_DIM)
        scores = lax.dot_general(
            query, key, (((1,), (1,)), ((), ())), preferred_element_type=f32
        ) * HEAD_DIM ** (-0.5)
        row = start * ROWS + lax.broadcasted_iota(jnp.int32, (Q_BLOCK, 1), 0)
        column = low * ROWS + lax.broadcasted_iota(jnp.int32, (Q_BLOCK, width), 1)
        begin = jnp.where(row < first, 0, jnp.where(row < second, first, second))
        allowed = (column <= row) & (column >= begin)
        scores = jnp.where(allowed, scores, NEG_FILL)
        top = jnp.max(scores, axis=-1, keepdims=True)
        probs = jnp.exp(scores - top)
        total = jnp.sum(probs, axis=-1, keepdims=True)
        mixed = jnp.dot(probs.astype(bf16), value, preferred_element_type=f32)
        out_ref[start:high] = (mixed / total).astype(bf16).reshape(per, ROWS, HEAD_DIM)


def place_of(expert):
    return (expert & 48) | (8 - (expert & 8)) | ((expert & 3) << 1) | ((expert >> 2) & 1)


def reach_of(expert, y):
    distance = (1 - ((expert >> 3) & 1) + ((expert >> 1) & 2) - y) & 3
    return (distance << 4) | ((expert >> 2) & 12) | (expert & 3)


def route_kernel(y_ref, ids_ref, codes_ref, pick_ref, weight_ref):
    number = lax.broadcasted_iota(jnp.int32, (EXPERTS, ROWS), 0)
    earlier = lax.broadcasted_iota(jnp.int32, (ROWS, ROWS), 0) < lax.broadcasted_iota(
        jnp.int32, (ROWS, ROWS), 1
    )
    earlier = jnp.where(earlier, 1.0, 0.0).astype(bf16)
    rows = EXPERTS * SLOTS
    own = lax.broadcasted_iota(jnp.int32, (rows, EXPERTS), 0) // SLOTS
    mine = own == lax.broadcasted_iota(jnp.int32, (rows, EXPERTS), 1)
    mine = jnp.where(mine, 1.0, 0.0).astype(bf16)
    slot = (lax.broadcasted_iota(jnp.int32, (rows, ROWS), 0) & (SLOTS - 1)) + 1
    ids = ids_ref[...]

    def ordered(names):
        member = jnp.zeros((EXPERTS, ROWS), f32)
        code = jnp.zeros((EXPERTS, ROWS), f32)
        for k in range(TOPK):
            named = number == names[k : k + 1, :]
            member = member + jnp.where(named, 1.0, 0.0)
            code = code + jnp.where(named, codes_ref[k : k + 1, :].astype(f32), 0.0)
        rank = jnp.dot(member.astype(bf16), earlier, preferred_element_type=f32)
        place = jnp.dot(mine, (member * (rank + 1.0)).astype(bf16), preferred_element_type=f32)
        return place == slot.astype(f32), code

    here, _ = ordered(reach_of(ids, y_ref[0]))
    pick_ref[...] = jnp.where(here, 1.0, 0.0).astype(bf16)
    here, code = ordered(place_of(ids))
    codes = jnp.dot(mine, code.astype(bf16), preferred_element_type=f32)
    weight_ref[...] = jnp.where(here, codes, 0.0).astype(bf16)


K_STEPS = 4


def project_kernel(heads_ref, weight_ref, hidden_ref, gain_ref, pick_ref, mixed_ref, *rest):
    shares, own_ref, acc = rest[:3], rest[3], rest[4]
    step = pl.program_id(0)
    per = HEADS // K_STEPS
    part = jnp.concatenate([heads_ref[i] for i in range(per)], axis=1)
    product = jnp.dot(part, weight_ref[...], preferred_element_type=f32)

    @pl.when(step == 0)
    def _():
        acc[...] = product
        for distance in range(1, Y_SIZE):
            for spot in range(SPOTS):
                lanes = slice(spot * ROWS, (spot + 1) * ROWS)
                first = (distance * SPOTS + spot) * SLOTS
                shares[distance - 1][ROWS:, lanes] = pick_ref[first : first + SLOTS, :]

    @pl.when(step > 0)
    def _():
        acc[...] += product

    @pl.when(step == K_STEPS - 1)
    def _():
        mixed = (hidden_ref[...].astype(f32) + acc[...]).astype(bf16)
        mixed_ref[...] = mixed
        wide = mixed.astype(f32)
        scale = lax.rsqrt(jnp.mean(wide * wide, axis=-1, keepdims=True) + 1e-06)
        normed = (wide * scale * gain_ref[...]).astype(bf16)
        for share_ref in shares:
            share_ref[0:ROWS, :] = normed
        picked = jnp.dot(pick_ref[: SPOTS * SLOTS, :], normed, preferred_element_type=f32)
        own_ref[...] = picked.astype(bf16).reshape(SPOTS, SLOTS, D)


def fill_kernel(near_ref, far_ref, back_ref, send_ref, rows, sems):
    copies = []
    for source, share_ref in enumerate((near_ref, back_ref, far_ref)):
        picks = [share_ref[ROWS:, i * ROWS : (i + 1) * ROWS] for i in range(SPOTS)]
        picked = jnp.dot(
            jnp.concatenate(picks, axis=0), share_ref[0:ROWS, :], preferred_element_type=f32
        )
        rows[source] = picked.astype(bf16).reshape(SPOTS, SLOTS, D)
        copy = pltpu.make_async_copy(rows.at[source], send_ref.at[:, source], sems.at[source])
        copy.start()
        copies.append(copy)
    for copy in copies:
        copy.wait()


def origin(unit):
    if unit < SPOTS:
        return unit, 0
    return (unit - SPOTS) // 3, (3, 1, 2)[(unit - SPOTS) % 3]


def inner_kernel(early, rows_ref, *refs):
    pieces = len(PIECES)
    parts, (act, w_in, sems) = refs[:pieces], refs[pieces:]
    copies, start = [], 0
    for number, (part, count) in enumerate(zip(parts, PIECES)):
        goal = w_in.at[pl.ds(start, count)]
        copies.append(pltpu.make_async_copy(part, goal, sems.at[number]))
        start += count
    for copy in copies:
        copy.start()
    for copy in copies[: pieces - early]:
        copy.wait()
    depth = D - PIECES[-1]
    for block in range(rows_ref.shape[0] // X_BLOCK):
        span = slice(block * X_BLOCK, (block + 1) * X_BLOCK)
        if block == 0 and early:
            inner = jnp.dot(rows_ref[span, :depth], w_in[:depth, :], preferred_element_type=f32)
            copies[-1].wait()
            rows = rows_ref[span, depth:]
            inner = inner + jnp.dot(rows, w_in[depth:, :], preferred_element_type=f32)
        else:
            inner = jnp.dot(rows_ref[span, :], w_in[...], preferred_element_type=f32)
        gate = inner[:, :HALF]
        up = pltpu.roll(inner, HALF, axis=1)[:, :HALF]
        act[span, :] = (gate / (1.0 + jnp.exp(-gate)) * up).astype(bf16)


def down_kernel(y_ref, own_a, own_b, rest_a, rest_b, down_any, down_b, out_ref, down_a, sem):
    y = y_ref[0]
    load = pltpu.make_async_copy(down_any, down_a, sem)
    load.start()
    units = X_BLOCK // SLOTS
    for block in range(EXPERTS * SLOTS // X_BLOCK):
        act_a, act_b, first = (own_a, own_b, 0) if block == 0 else (rest_a, rest_b, block - 1)
        span = slice(first * X_BLOCK, (first + 1) * X_BLOCK)
        total = jnp.dot(act_b[span, :], down_b[...], preferred_element_type=f32)
        if block == 0:
            load.wait()
        total = total + jnp.dot(act_a[span, :], down_a[...], preferred_element_type=f32)
        total = total.astype(bf16)
        for near in range(units):
            spot, ahead = origin(block * units + near)
            from_y = (y + ahead) & 3
            rows = total[near * SLOTS : (near + 1) * SLOTS, :]
            out_ref[spot // 4, from_y & 1, spot % 4, from_y >> 1] = rows


def combine_kernel(rows_ref, weight_ref, mixed_ref, out_ref):
    over = (((0,), (0,)), ((), ()))
    weight = weight_ref[...]
    routed = lax.dot_general(weight, rows_ref[...], over, preferred_element_type=f32)
    ones = jnp.ones((weight.shape[0], ROWS), bf16)
    total = lax.dot_general(weight, ones, over, preferred_element_type=f32)
    out_ref[...] = (mixed_ref[...].astype(f32) + routed / total[:, 0:1]).astype(bf16)


def local(
    queries,
    keys,
    values,
    segment_ids,
    hidden_in,
    out_weight,
    norm_gain,
    expert_ids,
    gate_codes,
    w_in,
    w_down,
):
    shape = jax.ShapeDtypeStruct
    y = (lax.axis_index("yl") + 2 * lax.axis_index("yh")).astype(jnp.int32)[None]
    gate_up, start, moved, other = w_in[0], 0, [], []
    for count in PIECES:
        piece = lax.slice_in_dim(gate_up, start, start + count)
        moved.append(lax.ppermute(piece, AXES, moves(weight_target)))
        other.append(lax.ppermute(moved[-1], AXES, moves(core_target)))
        start += count
    moved_down = lax.ppermute(w_down[0], AXES, moves(weight_target))
    other_down = lax.ppermute(moved_down, AXES, moves(core_target))
    packed = pl.pallas_call(
        pack_kernel,
        out_shape=shape((HEADS, PACK_ROWS, HEAD_DIM), bf16),
        in_specs=[VMEM] * 4,
        out_specs=VMEM,
        compiler_params=params(60),
        name="pack",
    )(queries[0], keys[0], values[0], segment_ids)
    swapped = lax.all_to_all(packed, POSITIONS, split_axis=0, concat_axis=0, tiled=True)
    attended = pl.pallas_call(
        attend_kernel,
        out_shape=shape((HEADS, ROWS, HEAD_DIM), bf16),
        in_specs=[VMEM],
        out_specs=VMEM,
        compiler_params=params(40),
        name="attend",
    )(swapped)
    heads = lax.all_to_all(attended, POSITIONS, split_axis=0, concat_axis=0, tiled=True)
    pick, weight = pl.pallas_call(
        route_kernel,
        out_shape=(
            shape((EXPERTS * SLOTS, ROWS), bf16),
            shape((EXPERTS * SLOTS, ROWS), bf16),
        ),
        in_specs=[SMEM, VMEM, VMEM],
        out_specs=(VMEM, VMEM),
        compiler_params=params(60),
        name="route",
    )(y, expert_ids[0].T, gate_codes[0].T)
    per = HEADS // K_STEPS
    share_shape = (ROWS + SLOTS, D)
    mixed, *shares, own = pl.pallas_call(
        project_kernel,
        grid=(K_STEPS,),
        out_shape=(
            shape((ROWS, D), bf16),
            shape(share_shape, bf16),
            shape(share_shape, bf16),
            shape(share_shape, bf16),
            shape((SPOTS, SLOTS, D), bf16),
        ),
        in_specs=[
            pl.BlockSpec((per, ROWS, HEAD_DIM), lambda i: (i, 0, 0)),
            pl.BlockSpec((D // K_STEPS, D), lambda i: (i, 0)),
            pl.BlockSpec((ROWS, D), lambda i: (0, 0)),
            pl.BlockSpec((1, D), lambda i: (0, 0)),
            pl.BlockSpec((EXPERTS * SLOTS, ROWS), lambda i: (0, 0)),
        ],
        out_specs=(
            pl.BlockSpec((ROWS, D), lambda i: (0, 0)),
            pl.BlockSpec(share_shape, lambda i: (0, 0)),
            pl.BlockSpec(share_shape, lambda i: (0, 0)),
            pl.BlockSpec(share_shape, lambda i: (0, 0)),
            pl.BlockSpec((SPOTS, SLOTS, D), lambda i: (0, 0, 0)),
        ),
        scratch_shapes=[pltpu.VMEM((ROWS, D), f32)],
        compiler_params=params(50),
        name="project",
    )(heads, out_weight, hidden_in[0], norm_gain[None], pick)
    arriving = []
    for distance, share in enumerate(shares, 1):
        arriving.append(lax.ppermute(share, AXES, moves(along_y(distance))))
    arrived_own = lax.all_to_all(own, ("z", "x"), split_axis=0, concat_axis=0, tiled=True)
    near, far, back = arriving
    send = pl.pallas_call(
        fill_kernel,
        out_shape=shape((SPOTS, 3, SLOTS, D), bf16),
        in_specs=[VMEM] * 3,
        out_specs=pl.BlockSpec(memory_space=pl.ANY),
        scratch_shapes=[
            pltpu.VMEM((3, SPOTS, SLOTS, D), bf16),
            pltpu.SemaphoreType.DMA((3,)),
        ],
        compiler_params=params(50),
        name="fill",
    )(near, far, back)
    arrived = lax.all_to_all(
        send.reshape(SPOTS, 3 * SLOTS, D), ("z", "x"), split_axis=0, concat_axis=0, tiled=True
    )
    anywhere = pl.BlockSpec(memory_space=pl.ANY)

    def inner(name, rows, parts):
        rows = rows.reshape(-1, D)
        return pl.pallas_call(
            functools.partial(inner_kernel, name == "rest_a"),
            out_shape=shape((rows.shape[0], HALF), bf16),
            in_specs=[VMEM] + [anywhere] * len(PIECES),
            out_specs=VMEM,
            scratch_shapes=[
                pltpu.VMEM((D, 2 * HALF), bf16),
                pltpu.SemaphoreType.DMA((len(PIECES),)),
            ],
            compiler_params=params(32),
        )(rows, *parts)

    own_a = inner("own_a", arrived_own, moved)
    own_b = inner("own_b", arrived_own, other)
    rest_a = inner("rest_a", arrived, moved)
    rest_b = inner("rest_b", arrived, other)
    results = pl.pallas_call(
        down_kernel,
        out_shape=shape((4, 2, 4, 2, SLOTS, D), bf16),
        in_specs=[SMEM] + [VMEM] * 4 + [anywhere, VMEM],
        out_specs=VMEM,
        scratch_shapes=[pltpu.VMEM((HALF, D), bf16), pltpu.SemaphoreType.DMA],
        compiler_params=params(32),
        name="down",
    )(y, own_a, own_b, rest_a, rest_b, moved_down, other_down)
    returned = lax.all_to_all(
        results.reshape(EXPERTS, SLOTS, D), PLACES, split_axis=0, concat_axis=0, tiled=True
    )
    layer_out = pl.pallas_call(
        combine_kernel,
        out_shape=shape((ROWS, D), bf16),
        in_specs=[VMEM] * 3,
        out_specs=VMEM,
        compiler_params=params(24),
        name="combine",
    )(returned.reshape(EXPERTS * SLOTS, D), weight, mixed)
    return layer_out[None]


def solution(mesh):
    parts = Mesh(mesh.devices.reshape(SIZES), AXES)
    rows = P(STREAM, POSITIONS, None)
    owned = P((*POSITIONS, *STREAM), None, None)
    placed = (rows, rows, rows, P(STREAM, POSITIONS), rows, P(), P(), rows, rows, owned, owned)
    return jax.shard_map(local, mesh=parts, in_specs=placed, out_specs=rows, check_vma=False)
```
